32 devices in a mesh: dp: 4 (over x, core), ctx: 4 (over z), tensor: 2 (over y).
Axes of the slice: x: 2, y: 2, z: 4, core: 2. Of those that a mesh axis runs over, the one named last changes fastest.
Arguments:
- out_grad: bfloat16 [4, 1024, 4096], P('dp', ('ctx', 'tensor')), may hold values from -1 to 1
- prev_state: bfloat16 [4, 1024, 4096], P('dp', 'ctx', 'tensor'), may hold values from -6 to 6
- boundary: int32 [4, 1024], P('dp', 'ctx'), may hold values 0 or 1
- angle_code: int32 [64, 32], P('tensor'), may hold values from 0 to 4095
- radius_code: int32 [64, 32], P('tensor'), may hold values from 0 to 1023
- reflect: float32 [64, 4, 64], P('tensor'), may hold values from -6 to 6
Outputs:
- grad_input: bfloat16 [4, 1024, 4096], P('dp', 'ctx', 'tensor')
- grad_transition: float32 [64, 64, 64], P('tensor')
The draws below stay inside these ranges and needn't reach their ends.
All inputs are finite; a program needn't handle non-finite values. No bound on the sum of `boundary` on one device may be relied on, other than what follows from the above.
Results may differ from the reference program's by a relative error of at most 0.003.
Values may be sent and summed in bfloat16 or wider, within the bound.
No kernel may reach another device: no remote copies, remote signals or barrier semaphores. Data moves between devices by JAX's collectives and lax.ppermute only.
A program may use at most 128 MiB of HBM per device.

```python
import math
import jax
import jax.numpy as jnp
from jax import lax

BLOCKS = 64
BSIZE = 64
TOK_DEV = 256
WIDTH = 4096
SEQLEN = 1024
NSEQ = 4
N_CTX = 4


def touch_ends(values, rng, least, largest):
    longest = values.shape.index(max(values.shape))
    spots = []
    for shift in (0, 1):
        where = [jax.random.randint(jax.random.fold_in(rng, axis), (), 0, length) for axis, length in enumerate(values.shape)]
        where[longest] = (where[longest] + shift) % values.shape[longest]
        spots.append(tuple(where))
    return values.at[spots[0]].set(least).at[spots[1]].set(largest)


def steps_of(stream_key, dims, pieces, least, high):
    factor_of, own = 1.0, jax.random.fold_in(stream_key, 6)
    for position, parts in pieces:
        draws = jnp.exp(jax.random.uniform(jax.random.fold_in(own, position), (parts,), jnp.float32, least / len(pieces), high / len(pieces)))
        factor_of = factor_of * jnp.repeat(draws, dims[position] // parts).reshape([-1 if axis == position else 1 for axis in range(len(dims))])
    return factor_of


def normal_values(stream_key, extent, deviation, bound, pieces=(), kind=jnp.bfloat16):
    level = steps_of(stream_key, extent, pieces, -0.22, 0.18) if pieces else 1.0
    entries = jax.random.normal(stream_key, extent, jnp.float32) * deviation * level
    return jnp.minimum(jnp.maximum(entries, -bound), bound).astype(kind)


def setup_inputs(seed: int = 0) -> dict:
    key_list = jax.random.split(jax.random.key(seed), 7)
    out_grad = normal_values(key_list[0], (NSEQ, SEQLEN, WIDTH), 0.125, 1.0, ((0, 4), (1, 8)))
    prev_state = normal_values(key_list[1], (NSEQ, SEQLEN, WIDTH), 1.0, 6.0, ((0, 4), (1, 4), (2, 2)))
    boundary = touch_ends((jax.random.randint(key_list[2], (NSEQ, SEQLEN), 0, TOK_DEV * N_CTX // 4) < 1).astype(jnp.int32), jax.random.fold_in(key_list[2], 1), 0, 1)
    angle_code = touch_ends(jax.random.randint(key_list[3], (BLOCKS, BSIZE // 2), 0, 4096), jax.random.fold_in(key_list[3], 1), 0, 4095).astype(jnp.int32)
    radius_code = touch_ends(jax.random.randint(key_list[4], (BLOCKS, BSIZE // 2), 0, 1024), jax.random.fold_in(key_list[4], 1), 0, 1023).astype(jnp.int32)
    reflect = normal_values(key_list[5], (BLOCKS, 4, BSIZE), 1.0, 6.0, ((0, 2),), jnp.float32)
    return dict(out_grad=out_grad, prev_state=prev_state, boundary=boundary, angle_code=angle_code, radius_code=radius_code, reflect=reflect)


def transition(angle_code, radius_code, reflect):
    block_count = radius_code.shape[0]
    block_size = 2 * radius_code.shape[1]
    rates = jnp.exp2(-(4.0 + radius_code.astype(jnp.float32) * (10.0 / 1024.0)))
    radius = 1.0 - rates
    angles = angle_code.astype(jnp.float32) * (math.pi / 4096.0)
    cosine = jnp.repeat(radius * jnp.cos(angles), 2, axis=1)[:, :, None]
    sine_part = jnp.repeat(radius * jnp.sin(angles), 2, axis=1)[:, :, None]
    row_index = jnp.arange(block_size)[:, None]
    col_index = jnp.arange(block_size)[None, :]
    on_diagonal = row_index == col_index
    upper_pair = (row_index % 2 == 0) & (col_index == row_index + 1)
    lower_pair = (row_index % 2 == 1) & (col_index == row_index - 1)
    zero_value = jnp.float32(0.0)
    rotation = jnp.where(on_diagonal[None], cosine, zero_value) + jnp.where(upper_pair[None], -sine_part, zero_value) + jnp.where(lower_pair[None], sine_part, zero_value)
    basis_now = jnp.broadcast_to(jnp.eye(block_size, dtype=jnp.float32), (block_count, block_size, block_size))
    for reflect_index in range(4):
        reflector = reflect[:, reflect_index, :].astype(jnp.float32)
        norm_sq = jnp.sum(reflector * reflector, axis=1)
        projected = jnp.einsum('bij,bj->bi', basis_now, reflector, precision=lax.Precision.HIGHEST)
        basis_now = basis_now - 2.0 * projected[:, :, None] * reflector[:, None, :] / norm_sq[:, None, None]
    rotated = jnp.einsum('bij,bjk->bik', basis_now, rotation, precision=lax.Precision.HIGHEST)
    return jnp.einsum('bik,blk->bil', rotated, basis_now, precision=lax.Precision.HIGHEST)


def reference(out_grad, prev_state, boundary, angle_code, radius_code, reflect):
    transit = transition(angle_code, radius_code, reflect)
    sequences, length, width_all = out_grad.shape
    grad_rows = out_grad.astype(jnp.float32).reshape(sequences, length, BLOCKS, BSIZE)
    previous = prev_state.astype(jnp.float32).reshape(sequences, length, BLOCKS, BSIZE)
    retain = jnp.where(boundary == 1, jnp.float32(0.6), jnp.float32(1.0)).astype(jnp.float32)

    def advance(state_pair, inputs):
        adjoint_next, accumulated = state_pair
        grad_row, prev_row, keep_row = inputs
        adjoint = grad_row + keep_row[:, None, None] * jnp.einsum('bji,sbj->sbi', transit, adjoint_next, precision=lax.Precision.HIGHEST)
        accumulated = accumulated + jnp.einsum('sbi,sbj->bij', adjoint, prev_row, precision=lax.Precision.HIGHEST)
        return (adjoint, accumulated), adjoint.astype(jnp.bfloat16)

    initial = (jnp.zeros((sequences, BLOCKS, BSIZE), jnp.float32), jnp.zeros((BLOCKS, BSIZE, BSIZE), jnp.float32))
    sequence_inputs = (jnp.swapaxes(grad_rows, 0, 1), jnp.swapaxes(previous, 0, 1), jnp.swapaxes(retain, 0, 1))
    (final_adjoint, grad_transition), outputs = lax.scan(advance, initial, sequence_inputs, reverse=True)
    grad_input = jnp.swapaxes(outputs, 0, 1).reshape(sequences, length, width_all)
    return grad_input, grad_transition
```

```python
import functools
import math

import jax
import jax.numpy as jnp
from jax import lax
from jax.experimental import pallas as pl
from jax.experimental.pallas import tpu as pltpu
from jax.sharding import PartitionSpec as P

F32 = jnp.float32
BF16 = jnp.bfloat16
LANES = 128
CHUNKS = 8
GROUP = 256
SIZE = 64


def iota(shape, dim):
    return lax.broadcasted_iota(jnp.int32, shape, dim)


def matmul(a, b, dims, precision=None):
    return lax.dot_general(a, b, (dims, ((), ())), precision=precision, preferred_element_type=F32)


def split(x):
    high = x.astype(BF16)
    return high, (x - high.astype(F32)).astype(BF16)


def setup_kernel(length, reflect_ref, angle_ref, radius_ref, keep_ref, high_ref, low_ref, tab_ref, hop_ref, ktab_ref, u_ref):
    step = pl.program_id(0)
    rows = reflect_ref.shape[0]
    blocks = rows // 4

    @pl.when(step == 0)
    def _():
        v = [reflect_ref[pl.ds(k, blocks, stride=4), :] for k in range(4)]
        u = []
        for k in range(4):
            now = v[k]
            for l in range(k):
                now = now - u[l] * jnp.sum(v[l] * v[k], axis=1, keepdims=True)
            u.append(now * (2.0 / jnp.sum(v[k] * v[k], axis=1, keepdims=True)))
        for k in range(4):
            u_ref[pl.ds(k, blocks, stride=4), :] = u[k]
        chunk = keep_ref[pl.ds(0, CHUNKS, stride=length), :]
        for i in range(1, length):
            chunk = chunk * keep_ref[pl.ds(i, CHUNKS, stride=length), :]
        row = iota((CHUNKS, LANES), 0)

        def later(x, k):
            return jnp.where(row < CHUNKS - k, pltpu.roll(x, CHUNKS - k, 0), 1.0)

        def earlier(x, k):
            return jnp.where(row >= k, pltpu.roll(x, k, 0), 1.0)

        two = chunk * later(chunk, 1)
        four = two * later(two, 2)
        before = earlier(chunk, 1)
        before = before * earlier(before, 1)
        before = before * earlier(before, 2)
        before = before * earlier(before, 4)
        eight = four * later(four, 4)
        ktab_ref[0] = chunk
        ktab_ref[1] = two
        ktab_ref[2] = four
        ktab_ref[3] = before
        ktab_ref[4] = jnp.broadcast_to(eight[0:1], (CHUNKS, LANES))

    width = GROUP
    own = iota((16, width), 0) // 4 == iota((16, width), 1) // SIZE
    at = pl.ds(pl.multiple_of(step * 16, 16), 16)
    v16 = reflect_ref[at, :]
    u16 = u_ref[at, :]
    v16 = jnp.where(own, jnp.concatenate([v16] * 4, axis=1), 0.0)
    u16 = jnp.where(own, jnp.concatenate([u16] * 4, axis=1), 0.0)
    column = iota((width, width), 1)
    half = column // LANES
    inside = column % LANES
    source = (inside // 32) * SIZE + (inside % 32) * 2 + half
    order = jnp.where(iota((width, width), 0) == source, 1.0, 0.0).astype(F32)
    v16 = matmul(v16, order, ((1,), (0,)), lax.Precision.HIGHEST)
    basis = order - matmul(u16, v16, ((0,), (0,)), lax.Precision.HIGHEST)
    high, low = split(basis)
    high_ref[0] = high
    low_ref[0] = low

    code = angle_ref[0]
    rate = jnp.exp(-math.log(2.0) * (4.0 + radius_ref[0].astype(F32) * (10.0 / 1024.0)))
    series = jnp.full_like(rate, 1.0 / 8.0)
    for n in range(7, 0, -1):
        series = series * rate + 1.0 / n
    log_radius = -rate * series

    def power(n):
        turn = ((n * code) & 8191).astype(F32) * (math.pi / 4096.0)
        size = jnp.exp(n.astype(F32) * log_radius)
        return size * jnp.cos(turn), -size * jnp.sin(turn)

    row = iota((CHUNKS, LANES), 0)
    n = jnp.where(row == 0, 1, jnp.where(row == 1, length, jnp.where(row == 2, 2 * length, jnp.where(row == 3, 4 * length, 8 * length))))
    re, im = power(n)
    tab_ref[0, 0] = re
    tab_ref[0, 1] = im
    re, im = power(row * length)
    hop_ref[0, 0] = re
    hop_ref[0, 1] = im


def setup(reflect, angle, radius, keep):
    blocks = reflect.shape[0]
    groups = blocks // 4
    tokens = keep.shape[0]
    whole = lambda shape: pl.BlockSpec(shape, lambda g: (0,) * len(shape))
    each = lambda shape: pl.BlockSpec((1,) + shape, lambda g: (g,) + (0,) * len(shape))
    return pl.pallas_call(
        functools.partial(setup_kernel, tokens // CHUNKS),
        grid=(groups,),
        in_specs=[whole((blocks * 4, SIZE)), each((1, LANES)), each((1, LANES)), whole((tokens, LANES))],
        out_specs=[
            each((GROUP, GROUP)),
            each((GROUP, GROUP)),
            each((2, CHUNKS, LANES)),
            each((2, CHUNKS, LANES)),
            whole((5, CHUNKS, LANES)),
        ],
        out_shape=[
            jax.ShapeDtypeStruct((groups, GROUP, GROUP), BF16),
            jax.ShapeDtypeStruct((groups, GROUP, GROUP), BF16),
            jax.ShapeDtypeStruct((groups, 2, CHUNKS, LANES), F32),
            jax.ShapeDtypeStruct((groups, 2, CHUNKS, LANES), F32),
            jax.ShapeDtypeStruct((5, CHUNKS, LANES), F32),
        ],
        scratch_shapes=[pltpu.VMEM((blocks * 4, SIZE), F32)],
        name="setup",
        cost_estimate=pl.CostEstimate(flops=groups * 60_000_000, bytes_accessed=groups * 300_000, transcendentals=groups * 10_000),
    )(reflect.reshape(blocks * 4, SIZE), angle.reshape(groups, 1, LANES), radius.reshape(groups, 1, LANES), keep)


def times(a, b):
    return a[0] * b[0] - a[1] * b[1], a[0] * b[1] + a[1] * b[0]


def first_kernel(length, peers, place_ref, *refs):
    own_ref, others, rest = refs[0], refs[1:peers], refs[peers:]
    high_ref, low_ref, tab_ref, hop_ref, ktab_ref, keep_ref, re_ref, im_ref, head_ref, first_ref, rows_ref = rest
    count = own_ref.shape[0]
    place = place_ref[0]
    rows_ref[pl.ds(pl.multiple_of(place * count, count), count), :] = own_ref[...]
    for k in range(1, peers):
        rows_ref[pl.ds(pl.multiple_of((place ^ k) * count, count), count), :] = others[k - 1][...]
    rows = rows_ref[...]
    out = matmul(rows, high_ref[0], ((1,), (0,))) + matmul(rows, low_ref[0], ((1,), (0,)))
    re_ref[...] = out[:, :LANES]
    im_ref[...] = out[:, LANES:]
    shape = (CHUNKS, LANES)
    unit = (jnp.broadcast_to(tab_ref[0, 0, 0:1], shape), jnp.broadcast_to(tab_ref[0, 1, 0:1], shape))
    at = pl.ds(length - 1, CHUNKS, stride=length)
    state = (re_ref[at, :], im_ref[at, :])
    for i in range(length - 2, -1, -1):
        at = pl.ds(i, CHUNKS, stride=length)
        keep = keep_ref[at, :]
        turned = times(unit, state)
        state = (re_ref[at, :] + keep * turned[0], im_ref[at, :] + keep * turned[1])
    head_ref[0, 0] = state[0]
    head_ref[0, 1] = state[1]
    moved = times((hop_ref[0, 0], hop_ref[0, 1]), state)
    before = ktab_ref[3]
    first_ref[0, 0] = jnp.sum(moved[0] * before, axis=0, keepdims=True)
    first_ref[0, 1] = jnp.sum(moved[1] * before, axis=0, keepdims=True)


def first_pass(place, parts, high, low, tab, hop, ktab, keep):
    peers = len(parts)
    count, channels = parts[0].shape
    groups = channels // GROUP
    tokens = keep.shape[0]
    each = lambda shape: pl.BlockSpec((1,) + shape, lambda g, *_: (g,) + (0,) * len(shape))
    whole = lambda shape: pl.BlockSpec(shape, lambda g, *_: (0,) * len(shape))
    columns = lambda n, w: pl.BlockSpec((n, w), lambda g, *_: (0, g))
    return pl.pallas_call(
        functools.partial(first_kernel, tokens // CHUNKS, peers),
        grid_spec=pltpu.PrefetchScalarGridSpec(
            num_scalar_prefetch=1,
            grid=(groups,),
            in_specs=[columns(count, GROUP)] * peers
            + [
                each((GROUP, GROUP)),
                each((GROUP, GROUP)),
                each((2, CHUNKS, LANES)),
                each((2, CHUNKS, LANES)),
                whole((5, CHUNKS, LANES)),
                whole((tokens, LANES)),
            ],
            out_specs=[columns(tokens, LANES), columns(tokens, LANES), each((2, CHUNKS, LANES)), each((2, 1, LANES))],
            scratch_shapes=[pltpu.VMEM((tokens, GROUP), BF16)],
        ),
        out_shape=[
            jax.ShapeDtypeStruct((tokens, groups * LANES), F32),
            jax.ShapeDtypeStruct((tokens, groups * LANES), F32),
            jax.ShapeDtypeStruct((groups, 2, CHUNKS, LANES), F32),
            jax.ShapeDtypeStruct((groups, 2, 1, LANES), F32),
        ],
        name="first_pass",
        cost_estimate=pl.CostEstimate(flops=groups * 70_000_000, bytes_accessed=groups * 700_000, transcendentals=0),
    )(place, *parts, high, low, tab, hop, ktab, keep)


def second_kernel(length, re_ref, im_ref, head_ref, entry_ref, high_ref, low_ref, tab_ref, ktab_ref, keep_ref, prev_ref, out_ref, grad_ref, zr_ref, zi_ref):
    shape = (CHUNKS, LANES)
    row = iota(shape, 0)
    table = lambda n: (jnp.broadcast_to(tab_ref[0, 0, n : n + 1], shape), jnp.broadcast_to(tab_ref[0, 1, n : n + 1], shape))
    entry = (jnp.broadcast_to(entry_ref[0, 0], shape), jnp.broadcast_to(entry_ref[0, 1], shape))
    moved = times(table(1), entry)
    last = row == CHUNKS - 1
    chunk = ktab_ref[0]
    scan = tuple(head_ref[0, c] + jnp.where(last, chunk * moved[c], 0.0) for c in range(2))
    for n in range(3):
        k = 1 << n
        near = tuple(jnp.where(row < CHUNKS - k, pltpu.roll(x, CHUNKS - k, 0), 0.0) for x in scan)
        moved = times(table(n + 1), near)
        scan = tuple(scan[c] + ktab_ref[n] * moved[c] for c in range(2))
    state = tuple(jnp.where(last, entry[c], pltpu.roll(scan[c], CHUNKS - 1, 0)) for c in range(2))
    unit = table(0)
    for i in range(length - 1, -1, -1):
        at = pl.ds(i, CHUNKS, stride=length)
        keep = keep_ref[at, :]
        turned = times(unit, state)
        state = (re_ref[at, :] + keep * turned[0], im_ref[at, :] + keep * turned[1])
        zr_ref[at, :] = state[0]
        zi_ref[at, :] = state[1]
    z_high, z_low = split(jnp.concatenate([zr_ref[...], zi_ref[...]], axis=1))
    contract = ((1,), (1,))
    adjoint = matmul(z_high, high_ref[0], contract) + matmul(z_high, low_ref[0], contract) + matmul(z_low, high_ref[0], contract)
    a_high, a_low = split(adjoint)
    out_ref[...] = a_high
    prev = prev_ref[...]
    grad = matmul(a_high, prev, ((0,), (0,))) + matmul(a_low, prev, ((0,), (0,)))
    left = iota((SIZE, LANES), 1) < SIZE
    for q in range(2):
        lanes = slice(q * LANES, (q + 1) * LANES)
        grad_ref[q * SIZE : (q + 1) * SIZE, :] = jnp.where(
            left, grad[q * LANES : q * LANES + SIZE, lanes], grad[q * LANES + SIZE : (q + 1) * LANES, lanes]
        )


def second_pass(re, im, head, entry, high, low, tab, ktab, keep, prev):
    tokens, channels = prev.shape
    groups = channels // GROUP
    each = lambda shape: pl.BlockSpec((1,) + shape, lambda g: (g,) + (0,) * len(shape))
    whole = lambda shape: pl.BlockSpec(shape, lambda g: (0,) * len(shape))
    columns = lambda n, w: pl.BlockSpec((n, w), lambda g: (0, g))
    return pl.pallas_call(
        functools.partial(second_kernel, tokens // CHUNKS),
        grid=(groups,),
        in_specs=[
            columns(tokens, LANES),
            columns(tokens, LANES),
            each((2, CHUNKS, LANES)),
            each((2, 1, LANES)),
            each((GROUP, GROUP)),
            each((GROUP, GROUP)),
            each((2, CHUNKS, LANES)),
            whole((5, CHUNKS, LANES)),
            whole((tokens, LANES)),
            columns(tokens, GROUP),
        ],
        out_specs=[columns(tokens, GROUP), pl.BlockSpec((2 * SIZE, LANES), lambda g: (g, 0))],
        out_shape=[
            jax.ShapeDtypeStruct((tokens, channels), BF16),
            jax.ShapeDtypeStruct((groups * 2 * SIZE, LANES), F32),
        ],
        scratch_shapes=[pltpu.VMEM((tokens, LANES), F32), pltpu.VMEM((tokens, LANES), F32)],
        name="second_pass",
        cost_estimate=pl.CostEstimate(flops=groups * 180_000_000, bytes_accessed=groups * 900_000, transcendentals=0),
    )(re, im, head, entry, high, low, tab, ktab, keep, prev)


def unpack_kernel(x_ref, o_ref):
    for n in range(x_ref.shape[0] // SIZE):
        rows = x_ref[n * SIZE : (n + 1) * SIZE, :]
        o_ref[2 * n] = rows[:, :SIZE]
        o_ref[2 * n + 1] = rows[:, SIZE:]


def unpack(x):
    blocks = x.shape[0] // SIZE * 2
    return pl.pallas_call(
        unpack_kernel, out_shape=jax.ShapeDtypeStruct((blocks, SIZE, SIZE), F32), name="unpack"
    )(x)


def swap(x, axis, k):
    n = lax.axis_size(axis)
    return lax.ppermute(x, axis, [(i, i ^ k) for i in range(n)])


def entering(first, total, far, axis):
    peers, place = lax.axis_size(axis), lax.axis_index(axis)
    entry = (jnp.zeros_like(first[0]), jnp.zeros_like(first[1]))
    gap = (jnp.ones_like(first[0]), jnp.zeros_like(first[0]))
    k = 1
    while k < peers:
        rows = first[0].shape[0]
        got = swap(jnp.concatenate([first[0], first[1], jnp.broadcast_to(total, (8, LANES))]), axis, k)
        other = (got[:rows], got[rows : 2 * rows])
        other_total = got[2 * rows : 2 * rows + 1]
        early = (place // k) % 2 == 0
        reach = times(gap, other)
        entry = tuple(jnp.where(early, e + r, e) for e, r in zip(entry, reach))
        if 2 * k < peers:
            step = times(gap, far)
            gap = tuple(jnp.where(early, other_total * s, g) for s, g in zip(step, gap))
            near = tuple(jnp.where(early, a, b) for a, b in zip(first, other))
            late = tuple(jnp.where(early, b, a) for a, b in zip(first, other))
            moved = times(far, late)
            first = tuple(a + jnp.where(early, total, other_total) * b for a, b in zip(near, moved))
            total = total * other_total
            far = times(far, far)
        k *= 2
    return entry


def total_sum(x, axes):
    steps = []
    for axis in axes:
        k = 1
        while k < lax.axis_size(axis):
            steps.append((axis, k))
            k *= 2
    done = []
    for axis, k in steps[:-1]:
        bit = (lax.axis_index(axis) // k) % 2
        m = x.shape[0] // 2
        away = lax.dynamic_slice_in_dim(x, (1 - bit) * m, m, 0)
        x = lax.dynamic_slice_in_dim(x, bit * m, m, 0) + swap(away, axis, k)
        done.append((axis, k, bit))
    axis, k = steps[-1]
    x = x + swap(x, axis, k)
    for axis, k, bit in done[::-1]:
        other = swap(x, axis, k)
        x = jnp.where(bit == 0, jnp.concatenate([x, other]), jnp.concatenate([other, x]))
    return x


def body(out_grad, prev_state, boundary, angle_code, radius_code, reflect):
    peers, place = lax.axis_size("tensor"), lax.axis_index("tensor")
    rows = out_grad[0]
    channels = prev_state.shape[2]
    tokens = prev_state.shape[1]
    part = lambda at: lax.dynamic_slice_in_dim(rows, at * channels, channels, 1)
    parts = [part(place)] + [swap(part(place ^ k), "tensor", k) for k in range(1, peers)]
    keep = jnp.where(boundary[0] == 1, F32(0.6), F32(1.0))
    keep = jnp.broadcast_to(keep[:, None], (tokens, LANES))
    high, low, tab, hop, ktab = setup(reflect, angle_code, radius_code, keep)
    re, im, head, first = first_pass(jnp.reshape(place, (1,)), parts, high, low, tab, hop, ktab, keep)
    far = (tab[:, 0, 4], tab[:, 1, 4])
    entry = entering((first[:, 0, 0], first[:, 1, 0]), ktab[4, :1], far, "ctx")
    entry = jnp.stack(entry, axis=1)[:, :, None, :]
    grad_input, partial = second_pass(re, im, head, entry, high, low, tab, ktab, keep, prev_state[0])
    summed = unpack(total_sum(partial, ("dp", "ctx")))
    return grad_input[None], summed


def solution(mesh):
    in_specs = (
        P("dp", ("ctx", "tensor"), None),
        P("dp", "ctx", "tensor"),
        P("dp", "ctx"),
        P("tensor", None),
        P("tensor", None),
        P("tensor", None, None),
    )
    out_specs = (P("dp", "ctx", "tensor"), P("tensor", None, None))
    return jax.shard_map(body, mesh=mesh, in_specs=in_specs, out_specs=out_specs, check_vma=False)
```

```python
import functools
import math

import jax
import jax.numpy as jnp
from jax import lax
from jax.experimental import pallas as pl
from jax.experimental.pallas import tpu as pltpu
from jax.sharding import PartitionSpec as P


F32 = jnp.float32
BF16 = jnp.bfloat16
LANES = 128
CHUNKS = 8
GROUP = 256
SIZE = 64
TILE = (CHUNKS, LANES)
LIMIT = 16 << 20
NN = ((1,), (0,))
NT = ((1,), (1,))
TN = ((0,), (0,))


def iota(shape, dim):
    return lax.broadcasted_iota(jnp.int32, shape, dim)


def matmul(a, b, dims=NN, precision=None):
    return lax.dot_general(a, b, (dims, ((), ())), precision=precision, preferred_element_type=F32)


def split(x):
    high = x.astype(BF16)
    return high, (x - high.astype(F32)).astype(BF16)


def split3(x):
    high = x.astype(BF16)
    rest = x - high.astype(F32)
    middle = rest.astype(BF16)
    return high, middle, (rest - middle.astype(F32)).astype(BF16)


def times(a, b):
    return a[0] * b[0] - a[1] * b[1], a[0] * b[1] + a[1] * b[0]


def later(x, k, fill):
    return jnp.where(iota(TILE, 0) < CHUNKS - k, pltpu.roll(x, CHUNKS - k, 0), fill)


def earlier(x, k, fill):
    return jnp.where(iota(TILE, 0) >= k, pltpu.roll(x, k, 0), fill)


def power(tab_ref, g, n):
    return tuple(jnp.broadcast_to(tab_ref[g, c, n : n + 1], TILE) for c in range(2))


def entries(tab_ref, ktab_ref, g, head, entry):
    last = iota(TILE, 0) == CHUNKS - 1
    moved = times(power(tab_ref, g, 1), entry)
    scan = tuple(jnp.where(last, ktab_ref[0] * m, 0.0) for m in moved)
    if head is not None:
        scan = tuple(h + s for h, s in zip(head, scan))
    for n in range(3):
        near = tuple(later(x, 1 << n, 0.0) for x in scan)
        moved = times(power(tab_ref, g, 1 << n), near)
        scan = tuple(s + ktab_ref[n] * m for s, m in zip(scan, moved))
    return tuple(jnp.where(last, e, pltpu.roll(s, CHUNKS - 1, 0)) for e, s in zip(entry, scan))


def fold(x):
    block = (iota((SIZE, GROUP), 1) % LANES) // 32
    out = x[:SIZE]
    for j in range(1, 4):
        out = jnp.where(block == j, x[j * SIZE : (j + 1) * SIZE], out)
    return out


def walk(length, groups, units, states, keep_ref, load, store):
    for i in range(length - 1, -1, -1):
        at = pl.ds(i, CHUNKS, stride=length)
        keep = keep_ref[at, :]
        for n in range(groups):
            re, im = states[n]
            step_re, step_im = keep * units[n][0], keep * units[n][1]
            if load is None:
                states[n] = (step_re * re - step_im * im, step_re * im + step_im * re)
            else:
                a, b = load(n, at)
                states[n] = ((a + step_re * re) - step_im * im, (b + step_re * im) + step_im * re)
            if store is not None:
                store(n, at, states[n])
    return states


def prepare_kernel(length, reflect_ref, angle_ref, radius_ref, keep_ref, prev_hbm,
                   high_ref, low_ref, tab_ref, ktab_ref, far_ref, turned_ref, decay_ref, weight_ref, u_ref, prev_ref, prev_sem):
    fetch = pltpu.make_async_copy(prev_hbm, prev_ref, prev_sem)
    fetch.start()
    rows = reflect_ref.shape[0]
    blocks = rows // 4
    groups = blocks // 4

    chunk = keep_ref[pl.ds(0, CHUNKS, stride=length), :]
    for i in range(1, length):
        chunk = chunk * keep_ref[pl.ds(i, CHUNKS, stride=length), :]
    two = chunk * later(chunk, 1, 1.0)
    four = two * later(two, 2, 1.0)
    before = earlier(chunk, 1, 1.0)
    before = before * earlier(before, 1, 1.0)
    before = before * earlier(before, 2, 1.0)
    before = before * earlier(before, 4, 1.0)
    eight = four * later(four, 4, 1.0)
    ktab_ref[0] = chunk
    ktab_ref[1] = two
    ktab_ref[2] = four
    ktab_ref[3] = before
    ktab_ref[4] = jnp.broadcast_to(eight[0:1], TILE)

    row = iota(TILE, 0)
    n = jnp.where(row == 0, 1, row * length)
    for g in range(groups):
        code = angle_ref[g : g + 1, :]
        rate = jnp.exp(-math.log(2.0) * (4.0 + radius_ref[g : g + 1, :].astype(F32) * (10.0 / 1024.0)))
        series = jnp.full_like(rate, 1.0 / 8.0)
        for k in range(7, 0, -1):
            series = series * rate + 1.0 / k
        turn = ((n * code) & 8191).astype(F32) * (math.pi / 4096.0)
        size = jnp.exp(n.astype(F32) * (-rate * series))
        re, im = size * jnp.cos(turn), -size * jnp.sin(turn)
        tab_ref[g, 0] = re
        tab_ref[g, 1] = im
        half = (re[4:5], im[4:5])
        whole = times(half, half)
        far_ref[0, g : g + 1, :] = whole[0]
        far_ref[1, g : g + 1, :] = whole[1]

    v = [reflect_ref[pl.ds(k, blocks, stride=4), :] for k in range(4)]
    u = []
    for k in range(4):
        now = v[k]
        for l in range(k):
            now = now - u[l] * jnp.sum(v[l] * v[k], axis=1, keepdims=True)
        u.append(now * (2.0 / jnp.sum(v[k] * v[k], axis=1, keepdims=True)))
        u_ref[pl.ds(k, blocks, stride=4), :] = u[k]
    to = iota((SIZE, SIZE), 1)
    sort = jnp.where(iota((SIZE, SIZE), 0) == (to % 32) * 2 + to // 32, 1.0, 0.0).astype(F32)
    sorted_v = matmul(reflect_ref[...], sort, NN, lax.Precision.HIGHEST)
    wide = (rows, GROUP)
    block = (iota(wide, 0) // 4) % 4
    wide_v = jnp.concatenate([sorted_v[:, :32]] * 4 + [sorted_v[:, 32:]] * 4, axis=1)
    wide_v = split3(jnp.where(block == (iota(wide, 1) % LANES) // 32, wide_v, 0.0))
    wide_u = split3(jnp.where(block == iota(wide, 1) // SIZE, jnp.concatenate([u_ref[...]] * 4, axis=1), 0.0))
    to = iota((GROUP, GROUP), 1)
    order = jnp.where(iota((GROUP, GROUP), 0) == ((to % LANES) // 32) * SIZE + (to % 32) * 2 + to // LANES, 1.0, 0.0).astype(F32)
    for g in range(groups):
        at = slice(g * 16, (g + 1) * 16)
        left = jnp.concatenate([wide_u[n][at] for n in (0, 0, 1, 0, 1, 2)], axis=0)
        right = jnp.concatenate([wide_v[n][at] for n in (0, 1, 0, 2, 1, 0)], axis=0)
        high, low = split(order - matmul(left, right, TN))
        high_ref[g] = high
        low_ref[g] = low

    one, zero = jnp.ones(TILE, F32), jnp.zeros(TILE, F32)
    for first in range(0, groups, 4):
        some = range(first, min(first + 4, groups))
        states = [entries(tab_ref, ktab_ref, g, None, (one, zero)) for g in some]
        units = [power(tab_ref, g, 0) for g in some]

        def store(k, at, state):
            decay_ref[first + k, 0, at, :] = state[0]
            decay_ref[first + k, 1, at, :] = state[1]

        walk(length, len(some), units, states, keep_ref, None, store)
    fetch.wait()
    for g in range(groups):
        columns = slice(g * GROUP, (g + 1) * GROUP)
        turned = prev_ref[:, columns].T
        turned_ref[columns, :] = turned
        high, low = split(jnp.concatenate([decay_ref[g, 0], decay_ref[g, 1]], axis=1))
        weight_ref[g] = fold(matmul(turned, high) + matmul(turned, low))


VMEM = pl.BlockSpec(memory_space=pltpu.VMEM)
SMEM = pl.BlockSpec(memory_space=pltpu.SMEM)


def call(kernel, out_shape, args, specs, scratch=(), flops=0):
    shapes = [jax.ShapeDtypeStruct(s, t) for s, t in out_shape]
    moved = sum(a.size * a.dtype.itemsize for a in args) + sum(s.size * s.dtype.itemsize for s in shapes)
    return pl.pallas_call(
        kernel,
        out_shape=shapes,
        in_specs=specs,
        out_specs=[VMEM] * len(shapes),
        scratch_shapes=list(scratch),
        compiler_params=pltpu.CompilerParams(vmem_limit_bytes=LIMIT),
        cost_estimate=pl.CostEstimate(flops=int(flops), bytes_accessed=int(moved), transcendentals=0),
    )(*args)


def prepare(reflect, angle, radius, keep, prev):
    blocks = reflect.shape[0]
    groups = blocks // 4
    tokens, channels = prev.shape
    out = [
        ((groups, GROUP, GROUP), BF16),
        ((groups, GROUP, GROUP), BF16),
        ((groups, 2) + TILE, F32),
        ((5,) + TILE, F32),
        ((2, groups, LANES), F32),
        ((channels, tokens), BF16),
        ((groups, 2, tokens, LANES), F32),
        ((groups, SIZE, GROUP), F32),
    ]
    args = (reflect.reshape(blocks * 4, SIZE), angle.reshape(groups, LANES), radius.reshape(groups, LANES), keep, prev)
    return call(functools.partial(prepare_kernel, tokens // CHUNKS), out, args, [VMEM] * 4 + [pl.BlockSpec(memory_space=pl.ANY)],
                [pltpu.VMEM((blocks * 4, SIZE), F32), pltpu.VMEM((tokens, channels), BF16), pltpu.SemaphoreType.DMA], groups * 2 * 2 * 256**3)


def scan_kernel(length, base, count, peers, begin, finish, *refs):
    refs = list(refs)
    take = lambda n: [refs.pop(0) for _ in range(n)]
    tab_ref, ktab_ref, keep_ref = take(3)
    if begin:
        place_ref, own_ref, high_ref, low_ref = take(4)
        others = take(peers - 1)
    if begin and not finish:
        (ahead_ref,) = take(1)
    if finish:
        (turned_ref,) = take(1)
    if begin:
        out_ref, head_ref, first_ref = take(3) if not finish else take(1) + [None] + take(1)
    else:
        in_ref, head_ref, out_ref = take(3)
    if finish:
        (grad_ref,) = take(1)
    heads = []
    if begin:
        rows_ref, = take(1)
        spaced_ref = take(1)[0] if finish else out_ref
        size = own_ref.shape[0]
        width = count * GROUP
        place = place_ref[0]
        channels = high_ref.shape[0] * GROUP
        at = pl.ds(pl.multiple_of(place * size, size), size)
        rows_ref[at, :] = own_ref[:, pl.ds(pl.multiple_of(place * channels + base * GROUP, GROUP), width)]
        for k in range(1, peers):
            rows_ref[pl.ds(pl.multiple_of((place ^ k) * size, size), size), :] = others[k - 1][...]
        for n in range(count):
            rows = rows_ref[:, n * GROUP : (n + 1) * GROUP]
            out = matmul(rows, high_ref[base + n]) + matmul(rows, low_ref[base + n])
            spaced_ref[n, 0] = out[:, :LANES]
            spaced_ref[n, 1] = out[:, LANES:]
    else:
        spaced_ref = in_ref
    load = lambda n, at: (spaced_ref[n, 0, at, :], spaced_ref[n, 1, at, :])
    units = [power(tab_ref, base + n, 0) for n in range(count)]
    zero = jnp.zeros(TILE, F32)
    if begin and not finish:
        groups = base + count
        for c in range(2):
            first_ref[c * groups : c * groups + base, :] = ahead_ref[c]
        first_ref[2 * groups :, :] = ktab_ref[4]
    if begin:
        heads = walk(length, count, units, [(zero, zero)] * count, keep_ref, load, None)
        before = ktab_ref[3]
        for n in range(count):
            if head_ref is not None:
                head_ref[n, 0] = heads[n][0]
                head_ref[n, 1] = heads[n][1]
            hop = tuple(jnp.where(iota(TILE, 0) == 0, one, tab_ref[base + n, c]) for c, one in ((0, 1.0), (1, 0.0)))
            moved = times(hop, heads[n])
            for c in range(2):
                value = jnp.sum(moved[c] * before, axis=0, keepdims=True)
                if finish:
                    first_ref[c, n : n + 1, :] = value
                else:
                    first_ref[c * groups + base + n : c * groups + base + n + 1, :] = value
    else:
        heads = [(head_ref[n, 0], head_ref[n, 1]) for n in range(count)]
    if finish:
        states = [entries(tab_ref, ktab_ref, base + n, heads[n], (zero, zero)) for n in range(count)]

        def store(n, at, state):
            out_ref[n, 0, at, :] = state[0]
            out_ref[n, 1, at, :] = state[1]

        walk(length, count, units, states, keep_ref, load, store)
        for n in range(count):
            high, low = split(jnp.concatenate([out_ref[n, 0], out_ref[n, 1]], axis=1))
            turned = turned_ref[(base + n) * GROUP : (base + n + 1) * GROUP, :]
            grad_ref[n] = fold(matmul(turned, high) + matmul(turned, low))


def scan_both(base, count, place, rows, parts, high, low, tab, ktab, keep, turned):
    tokens = keep.shape[0]
    peers = len(parts) + 1
    out = [((count, 2, tokens, LANES), F32), ((2, count, LANES), F32), ((count, SIZE, GROUP), F32)]
    return call(functools.partial(scan_kernel, tokens // CHUNKS, base, count, peers, True, True), out,
                (tab, ktab, keep, place, rows, high, low, *parts, turned), [VMEM] * 3 + [SMEM] + [VMEM] * (peers + 3),
                [pltpu.VMEM((tokens, count * GROUP), BF16), pltpu.VMEM((count, 2, tokens, LANES), F32)], count * 4 * 2 * 256**3)


def scan_first(base, count, place, rows, parts, high, low, tab, ktab, keep, ahead):
    tokens = keep.shape[0]
    peers = len(parts) + 1
    out = [((count, 2, tokens, LANES), F32), ((count, 2) + TILE, F32), ((2 * (base + count) + CHUNKS, LANES), F32)]
    return call(functools.partial(scan_kernel, tokens // CHUNKS, base, count, peers, True, False), out,
                (tab, ktab, keep, place, rows, high, low, *parts, ahead), [VMEM] * 3 + [SMEM] + [VMEM] * (peers + 3),
                [pltpu.VMEM((tokens, count * GROUP), BF16)], count * 2 * 2 * 256**3)


def scan_second(base, count, spaced, head, tab, ktab, keep, turned):
    tokens = keep.shape[0]
    out = [((count, 2, tokens, LANES), F32), ((count, SIZE, GROUP), F32)]
    return call(functools.partial(scan_kernel, tokens // CHUNKS, base, count, 0, False, True), out,
                (tab, ktab, keep, turned, spaced, head), [VMEM] * 6, (), count * 2 * 2 * 256**3)


def merge_kernel(side_ref, a_ref, b_ref, weight_ref, entry_ref, own_ref, away_ref):
    half = a_ref.shape[0]
    side = side_ref[0]
    for n in range(half):
        for out_ref, which in ((own_ref, side), (away_ref, 1 - side)):
            here = jnp.where(which == 0, a_ref[n], b_ref[n])
            at = which * half + n
            re, im = entry_ref[0, pl.ds(at, 1), :], entry_ref[1, pl.ds(at, 1), :]
            weight = weight_ref[at]
            w_re, w_im = weight[:, :LANES], weight[:, LANES:]
            out_ref[n * SIZE : (n + 1) * SIZE, :LANES] = here[:, :LANES] + (re * w_re - im * w_im)
            out_ref[n * SIZE : (n + 1) * SIZE, LANES:] = here[:, LANES:] + (re * w_im + im * w_re)


def merge(side, a, b, weight, entry):
    rows = a.shape[0] * SIZE
    return call(merge_kernel, [((rows, GROUP), F32)] * 2, (side, a, b, weight, entry), [SMEM] + [VMEM] * 4)


def state_kernel(half, a_ref, b_ref, decay_ref, entry_ref, high_ref, low_ref, out_ref):
    g = pl.program_id(0)
    re, im = entry_ref[0, pl.ds(g, 1), :], entry_ref[1, pl.ds(g, 1), :]
    d_re, d_im = decay_ref[0, 0], decay_ref[0, 1]
    first = g < half
    z_re = jnp.where(first, a_ref[0, 0], b_ref[0, 0]) + (re * d_re - im * d_im)
    z_im = jnp.where(first, a_ref[0, 1], b_ref[0, 1]) + (re * d_im + im * d_re)
    z_high, z_low = split(jnp.concatenate([z_re, z_im], axis=1))
    out = matmul(z_high, high_ref[0], NT) + matmul(z_high, low_ref[0], NT) + matmul(z_low, high_ref[0], NT)
    out_ref[...] = out.astype(BF16)


def states(a, b, decay, entry, high, low):
    half, _, tokens, _ = a.shape
    groups = 2 * half
    each = lambda shape: pl.BlockSpec((1,) + shape, lambda g: (g, 0, 0, 0)[: len(shape) + 1])
    return pl.pallas_call(
        functools.partial(state_kernel, half),
        grid=(groups,),
        in_specs=[
            pl.BlockSpec((1, 2, tokens, LANES), lambda g: (jnp.minimum(g, half - 1), 0, 0, 0)),
            pl.BlockSpec((1, 2, tokens, LANES), lambda g: (jnp.maximum(g - half, 0), 0, 0, 0)),
            each((2, tokens, LANES)),
            pl.BlockSpec(entry.shape, lambda g: (0, 0, 0)),
            each((GROUP, GROUP)),
            each((GROUP, GROUP)),
        ],
        out_specs=pl.BlockSpec((tokens, GROUP), lambda g: (0, g)),
        out_shape=jax.ShapeDtypeStruct((tokens, groups * GROUP), BF16),
        name="states",
        compiler_params=pltpu.CompilerParams(vmem_limit_bytes=LIMIT),
        cost_estimate=pl.CostEstimate(flops=groups * 3 * 2 * 256**3, bytes_accessed=groups * 900_000, transcendentals=0),
    )(a, b, decay, entry, high, low)


def final_kernel(side_ref, own_ref, other_ref, high_ref, low_ref, out_ref):
    half = high_ref.shape[0] // 2
    side = side_ref[0]
    for x_ref, which in ((own_ref, side), (other_ref, 1 - side)):
        for n in range(half):
            at = which * half + n
            x_high, x_low = split(x_ref[n * SIZE : (n + 1) * SIZE, :])
            high = high_ref[at]
            out = matmul(high, x_high, NT) + matmul(high, x_low, NT) + matmul(low_ref[at], x_high, NT)
            for j in range(4):
                out_ref[at * 4 + j] = out[j * SIZE : (j + 1) * SIZE]


def final(side, own, other, high, low):
    blocks = high.shape[0] * 4
    return call(final_kernel, [((blocks, SIZE, SIZE), F32)], (side, own, other, high, low), [SMEM] + [VMEM] * 4)[0]


def swap(x, axis, k):
    n = lax.axis_size(axis)
    return lax.ppermute(x, axis, [(i, i ^ k) for i in range(n)])


def entering(sent, far, axis, early_bits):
    peers = lax.axis_size(axis)
    rows = far[0].shape[0]
    first, total = (sent[:rows], sent[rows : 2 * rows]), sent[2 * rows : 2 * rows + 1]
    entry = (jnp.zeros_like(first[0]), jnp.zeros_like(first[1]))
    gap = (jnp.ones_like(first[0]), jnp.zeros_like(first[0]))
    k = 1
    for early in early_bits:
        if k > 1:
            sent = jnp.concatenate([first[0], first[1], jnp.broadcast_to(total, (8, LANES))])
        got = swap(sent, axis, k)
        other = (got[:rows], got[rows : 2 * rows])
        other_total = got[2 * rows : 2 * rows + 1]
        reach = times(gap, other)
        entry = tuple(jnp.where(early, e + r, e) for e, r in zip(entry, reach))
        if 2 * k < peers:
            step = times(gap, far)
            gap = tuple(jnp.where(early, other_total * s, g) for s, g in zip(step, gap))
            near = tuple(jnp.where(early, a, b) for a, b in zip(first, other))
            late = tuple(jnp.where(early, b, a) for a, b in zip(first, other))
            moved = times(far, late)
            first = tuple(a + jnp.where(early, total, other_total) * b for a, b in zip(near, moved))
            total = total * other_total
            far = times(far, far)
        k *= 2
    return jnp.stack(entry)


def exchanges(axes):
    steps = []
    for axis in axes:
        k = 1
        while k < lax.axis_size(axis):
            steps.append((axis, k))
            k *= 2
    return steps


def bits(steps):
    return [(lax.axis_index(axis).astype(jnp.uint32) // jnp.uint32(k)) & jnp.uint32(1) for axis, k in steps]


def piece(x, start, size):
    return lax.dynamic_slice(x, (start, jnp.uint32(0)), (size, x.shape[1]))


def total_sum(own, away, steps, starts):
    x = own + swap(away, *steps[0])
    for (axis, k), (here, there, _) in zip(steps[1:-1], starts):
        m = x.shape[0] // 2
        x = piece(x, here, m) + swap(piece(x, there, m), axis, k)
    x = x + swap(x, *steps[-1])
    for (axis, k), (_, _, lower) in list(zip(steps[1:-1], starts))[::-1]:
        other = swap(x, axis, k)
        x = jnp.where(lower, jnp.concatenate([x, other]), jnp.concatenate([other, x]))
    return x, swap(x, *steps[0])


def inner(out_grad, prev_state, boundary, angle_code, radius_code, reflect):
    peers, place = lax.axis_size("tensor"), lax.axis_index("tensor")
    rows = out_grad[0]
    channels = prev_state.shape[2]
    tokens = prev_state.shape[1]
    groups = channels // GROUP
    half = groups // 2
    width = half * GROUP
    place = place.astype(jnp.uint32)

    def away(k, h):
        start = (place ^ jnp.uint32(k)) * jnp.uint32(channels) + jnp.uint32(h * width)
        return lax.dynamic_slice(rows, (jnp.uint32(0), start), (rows.shape[0], width))

    parts = [[swap(away(k, h), "tensor", k) for k in range(1, peers)] for h in range(2)]
    steps = exchanges(("dp", "ctx"))
    size = half * SIZE
    starts = []
    for bit in bits(steps)[1:-1]:
        size //= 2
        starts.append((bit * jnp.uint32(size), (jnp.uint32(1) - bit) * jnp.uint32(size), bit == 0))
    side = jnp.reshape(lax.axis_index("dp") & 1, (1,))
    place = jnp.reshape(place.astype(jnp.int32), (1,))
    early = [bit == 0 for bit in bits(exchanges(("ctx",)))]
    boundary, reflect, side, place, starts, early = lax.optimization_barrier((boundary, reflect, side, place, starts, early))
    keep = jnp.where(boundary[0] == 1, jnp.float32(0.6), jnp.float32(1.0))
    keep = jnp.broadcast_to(keep[:, None], (tokens, LANES))
    high, low, tab, ktab, far, turned, decay, weight = prepare(reflect, angle_code, radius_code, keep, prev_state[0])
    z_a, first_a, grad_a = scan_both(0, half, place, rows, parts[0], high, low, tab, ktab, keep, turned)
    spaced, head, sent = scan_first(half, half, place, rows, parts[1], high, low, tab, ktab, keep, first_a)
    entry = entering(sent, (far[0], far[1]), "ctx", early)
    z_b, grad_b = scan_second(half, half, spaced, head, tab, ktab, keep, turned)
    own, other = merge(side, grad_a, grad_b, weight, entry)
    grad_input = states(z_a, z_b, decay, entry, high, low)
    own, other = total_sum(own, other, steps, starts)
    return grad_input[None], final(side, own, other, high, low)


def solution(mesh):
    in_specs = (
        P("dp", ("ctx", "tensor"), None),
        P("dp", "ctx", "tensor"),
        P("dp", "ctx"),
        P("tensor", None),
        P("tensor", None),
        P("tensor", None, None),
    )
    out_specs = (P("dp", "ctx", "tensor"), P("tensor", None, None))
    return jax.shard_map(inner, mesh=mesh, in_specs=in_specs, out_specs=out_specs, check_vma=False)
```

```python
import functools
import math

import jax
import jax.numpy as jnp
from jax import lax
from jax.experimental import pallas as pl
from jax.experimental.pallas import tpu as pltpu
from jax.sharding import PartitionSpec as P


F32 = jnp.float32
BF16 = jnp.bfloat16
LANES = 128
CHUNKS = 8
GROUP = 256
SIZE = 64
TILE = (CHUNKS, LANES)
LIMIT = 16 << 20
NN = ((1,), (0,))
NT = ((1,), (1,))
TN = ((0,), (0,))


def iota(shape, dim):
    return lax.broadcasted_iota(jnp.int32, shape, dim)


def matmul(a, b, dims=NN, precision=None):
    return lax.dot_general(a, b, (dims, ((), ())), precision=precision, preferred_element_type=F32)


def split(x):
    high = x.astype(BF16)
    return high, (x - high.astype(F32)).astype(BF16)


def split3(x):
    high = x.astype(BF16)
    rest = x - high.astype(F32)
    middle = rest.astype(BF16)
    return high, middle, (rest - middle.astype(F32)).astype(BF16)


def times(a, b):
    return a[0] * b[0] - a[1] * b[1], a[0] * b[1] + a[1] * b[0]


def later(x, k, fill):
    return jnp.where(iota(TILE, 0) < CHUNKS - k, pltpu.roll(x, CHUNKS - k, 0), fill)


def earlier(x, k, fill):
    return jnp.where(iota(TILE, 0) >= k, pltpu.roll(x, k, 0), fill)


def power(tab_ref, g, n):
    return tuple(jnp.broadcast_to(tab_ref[g, c, n : n + 1], TILE) for c in range(2))


def entries(tab_ref, ktab_ref, g, head, entry):
    last = iota(TILE, 0) == CHUNKS - 1
    moved = times(power(tab_ref, g, 1), entry)
    scan = tuple(jnp.where(last, ktab_ref[0] * m, 0.0) for m in moved)
    if head is not None:
        scan = tuple(h + s for h, s in zip(head, scan))
    for n in range(3):
        near = tuple(later(x, 1 << n, 0.0) for x in scan)
        moved = times(power(tab_ref, g, 1 << n), near)
        scan = tuple(s + ktab_ref[n] * m for s, m in zip(scan, moved))
    return tuple(jnp.where(last, e, pltpu.roll(s, CHUNKS - 1, 0)) for e, s in zip(entry, scan))


def fold(x):
    block = (iota((SIZE, GROUP), 1) % LANES) // 32
    out = x[:SIZE]
    for j in range(1, 4):
        out = jnp.where(block == j, x[j * SIZE : (j + 1) * SIZE], out)
    return out


def walk(length, groups, units, states, keep_ref, load, store):
    for i in range(length - 1, -1, -1):
        at = pl.ds(i, CHUNKS, stride=length)
        keep = keep_ref[at, :]
        for n in range(groups):
            re, im = states[n]
            step_re, step_im = keep * units[n][0], keep * units[n][1]
            if load is None:
                states[n] = (step_re * re - step_im * im, step_re * im + step_im * re)
            else:
                a, b = load(n, at)
                states[n] = ((a + step_re * re) - step_im * im, (b + step_re * im) + step_im * re)
            if store is not None:
                store(n, at, states[n])
    return states


def basis_kernel(length, code_ref, reflect_ref, high_ref, low_ref, tab_ref, far_ref, u_ref, wide_ref):
    rows = reflect_ref.shape[0]
    blocks = rows // 4
    groups = blocks // 4

    wide_ref[...] = jnp.concatenate([code_ref[...]] * 4, axis=1)
    codes = wide_ref[pl.ds(0, groups, stride=4), :]
    block = iota(codes.shape, 1) // 32
    for j in range(1, 4):
        codes = jnp.where(block == j, wide_ref[pl.ds(j, groups, stride=4), :], codes)

    rates = jnp.exp(-math.log(2.0) * (4.0 + (codes & 1023).astype(F32) * (10.0 / 1024.0)))
    series = jnp.full_like(rates, 1.0 / 8.0)
    for k in range(7, 0, -1):
        series = series * rates + 1.0 / k
    logs = -rates * series
    angles = codes >> 10
    row = iota(TILE, 0)
    n = jnp.where(row == 0, 1, row * length)
    for g in range(groups):
        turn = ((n * angles[g : g + 1, :]) & 8191).astype(F32) * (math.pi / 4096.0)
        size = jnp.exp(n.astype(F32) * logs[g : g + 1, :])
        re, im = size * jnp.cos(turn), -size * jnp.sin(turn)
        tab_ref[g, 0] = re
        tab_ref[g, 1] = im
        half = (re[4:5], im[4:5])
        whole = times(half, half)
        far_ref[0, g : g + 1, :] = whole[0]
        far_ref[1, g : g + 1, :] = whole[1]

    v = [reflect_ref[pl.ds(k, blocks, stride=4), :] for k in range(4)]
    u = []
    for k in range(4):
        now = v[k]
        for l in range(k):
            now = now - u[l] * jnp.sum(v[l] * v[k], axis=1, keepdims=True)
        u.append(now * (2.0 / jnp.sum(v[k] * v[k], axis=1, keepdims=True)))
        u_ref[pl.ds(k, blocks, stride=4), :] = u[k]
    to = iota((SIZE, SIZE), 1)
    sort = jnp.where(iota((SIZE, SIZE), 0) == (to % 32) * 2 + to // 32, 1.0, 0.0).astype(F32)
    sorted_v = matmul(reflect_ref[...], sort, NN, lax.Precision.HIGHEST)
    wide = (rows, GROUP)
    block = (iota(wide, 0) // 4) % 4
    wide_v = jnp.concatenate([sorted_v[:, :32]] * 4 + [sorted_v[:, 32:]] * 4, axis=1)
    wide_v = split3(jnp.where(block == (iota(wide, 1) % LANES) // 32, wide_v, 0.0))
    wide_u = split3(jnp.where(block == iota(wide, 1) // SIZE, jnp.concatenate([u_ref[...]] * 4, axis=1), 0.0))
    to = iota((GROUP, GROUP), 1)
    order = jnp.where(iota((GROUP, GROUP), 0) == ((to % LANES) // 32) * SIZE + (to % 32) * 2 + to // LANES, 1.0, 0.0).astype(F32)
    for g in range(groups):
        at = slice(g * 16, (g + 1) * 16)
        left = jnp.concatenate([wide_u[n][at] for n in (0, 0, 1, 0, 1, 2)], axis=0)
        right = jnp.concatenate([wide_v[n][at] for n in (0, 1, 0, 2, 1, 0)], axis=0)
        high, low = split(order - matmul(left, right, TN))
        high_ref[g] = high
        low_ref[g] = low


def weight_kernel(length, boundary_ref, tab_ref, prev_ref, keep_ref, ktab_ref, turned_ref, decay_ref, weight_ref):
    groups = tab_ref.shape[0]
    keep = jnp.where(boundary_ref[...] == 1, 0.6, 1.0).astype(F32)
    keep_ref[...] = jnp.broadcast_to(keep, (LANES, keep.shape[1])).T

    chunk = keep_ref[pl.ds(0, CHUNKS, stride=length), :]
    for i in range(1, length):
        chunk = chunk * keep_ref[pl.ds(i, CHUNKS, stride=length), :]
    two = chunk * later(chunk, 1, 1.0)
    four = two * later(two, 2, 1.0)
    before = earlier(chunk, 1, 1.0)
    before = before * earlier(before, 1, 1.0)
    before = before * earlier(before, 2, 1.0)
    before = before * earlier(before, 4, 1.0)
    eight = four * later(four, 4, 1.0)
    ktab_ref[0] = chunk
    ktab_ref[1] = two
    ktab_ref[2] = four
    ktab_ref[3] = before
    ktab_ref[4] = jnp.broadcast_to(eight[0:1], TILE)

    one, zero = jnp.ones(TILE, F32), jnp.zeros(TILE, F32)
    for first in range(0, groups, 4):
        some = range(first, min(first + 4, groups))
        states = [entries(tab_ref, ktab_ref, g, None, (one, zero)) for g in some]
        units = [power(tab_ref, g, 0) for g in some]

        def store(k, at, state):
            decay_ref[first + k, 0, at, :] = state[0]
            decay_ref[first + k, 1, at, :] = state[1]

        walk(length, len(some), units, states, keep_ref, None, store)
    for g in range(groups):
        columns = slice(g * GROUP, (g + 1) * GROUP)
        turned = prev_ref[:, columns].T
        turned_ref[columns, :] = turned
        high, low = split(jnp.concatenate([decay_ref[g, 0], decay_ref[g, 1]], axis=1))
        weight_ref[g] = fold(matmul(turned, high) + matmul(turned, low))


VMEM = pl.BlockSpec(memory_space=pltpu.VMEM)
SMEM = pl.BlockSpec(memory_space=pltpu.SMEM)
HBM = pl.BlockSpec(memory_space=pltpu.HBM)


def call(kernel, out_shape, args, specs, scratch=(), flops=0):
    shapes = [jax.ShapeDtypeStruct(s, t) for s, t in out_shape]
    moved = sum(a.size * a.dtype.itemsize for a in args) + sum(s.size * s.dtype.itemsize for s in shapes)
    return pl.pallas_call(
        kernel,
        out_shape=shapes,
        in_specs=specs,
        out_specs=[VMEM] * len(shapes),
        scratch_shapes=list(scratch),
        compiler_params=pltpu.CompilerParams(vmem_limit_bytes=LIMIT),
        cost_estimate=pl.CostEstimate(flops=int(flops), bytes_accessed=int(moved), transcendentals=0),
    )(*args)


def basis(code, reflect, length):
    blocks = reflect.shape[0]
    groups = blocks // 4
    out = [
        ((groups, GROUP, GROUP), BF16),
        ((groups, GROUP, GROUP), BF16),
        ((groups, 2) + TILE, F32),
        ((2, groups, LANES), F32),
    ]
    args = (code, reflect.reshape(blocks * 4, SIZE))
    scratch = [pltpu.VMEM((blocks * 4, SIZE), F32), pltpu.VMEM((blocks, LANES), jnp.int32)]
    return call(functools.partial(basis_kernel, length), out, args, [VMEM] * 2, scratch, groups * 2 * 2 * 256**3)


def weights(boundary, tab, prev):
    groups = tab.shape[0]
    tokens, channels = prev.shape
    out = [
        ((tokens, LANES), F32),
        ((5,) + TILE, F32),
        ((channels, tokens), BF16),
        ((groups, 2, tokens, LANES), F32),
        ((groups, SIZE, GROUP), F32),
    ]
    return call(functools.partial(weight_kernel, tokens // CHUNKS), out, (boundary, tab, prev), [VMEM] * 3, (), groups * 2 * 2 * 256**3)


def scan_kernel(length, base, count, peers, begin, finish, aheads, *refs):
    refs = list(refs)
    take = lambda n: [refs.pop(0) for _ in range(n)]
    tab_ref, ktab_ref, keep_ref = take(3)
    if begin:
        place_ref, own_ref, high_ref, low_ref = take(4)
        others = take(peers - 1)
    if begin and not finish:
        ahead = take(aheads)
    if finish:
        (turned_ref,) = take(1)
    if begin:
        out_ref, head_ref, first_ref = take(3) if not finish else take(1) + [None] + take(1)
    else:
        in_ref, head_ref, out_ref = take(3)
    if finish:
        (grad_ref,) = take(1)
    heads = []
    if begin:
        rows_ref, = take(1)
        spaced_ref = take(1)[0] if finish else out_ref
        size = own_ref.shape[0]
        width = count * GROUP
        place = place_ref[0]
        channels = high_ref.shape[0] * GROUP
        at = pl.ds(pl.multiple_of(place * size, size), size)
        rows_ref[at, :] = own_ref[:, pl.ds(pl.multiple_of(place * channels + base * GROUP, GROUP), width)]
        for k in range(1, peers):
            rows_ref[pl.ds(pl.multiple_of((place ^ k) * size, size), size), :] = others[k - 1][...]
        for n in range(count):
            rows = rows_ref[:, n * GROUP : (n + 1) * GROUP]
            out = matmul(rows, high_ref[base + n]) + matmul(rows, low_ref[base + n])
            spaced_ref[n, 0] = out[:, :LANES]
            spaced_ref[n, 1] = out[:, LANES:]
    else:
        spaced_ref = in_ref
    load = lambda n, at: (spaced_ref[n, 0, at, :], spaced_ref[n, 1, at, :])
    units = [power(tab_ref, base + n, 0) for n in range(count)]
    zero = jnp.zeros(TILE, F32)
    if begin and not finish:
        groups = base + count
        at = 0
        for ref in ahead:
            size = ref.shape[1]
            for c in range(2):
                first_ref[c * groups + at : c * groups + at + size, :] = ref[c]
            at += size
        first_ref[2 * groups :, :] = ktab_ref[4]
    if begin:
        heads = walk(length, count, units, [(zero, zero)] * count, keep_ref, load, None)
        before = ktab_ref[3]
        for n in range(count):
            if head_ref is not None:
                head_ref[n, 0] = heads[n][0]
                head_ref[n, 1] = heads[n][1]
            hop = tuple(jnp.where(iota(TILE, 0) == 0, one, tab_ref[base + n, c]) for c, one in ((0, 1.0), (1, 0.0)))
            moved = times(hop, heads[n])
            for c in range(2):
                value = jnp.sum(moved[c] * before, axis=0, keepdims=True)
                if finish:
                    first_ref[c, n : n + 1, :] = value
                else:
                    first_ref[c * groups + base + n : c * groups + base + n + 1, :] = value
    else:
        heads = [(head_ref[n, 0], head_ref[n, 1]) for n in range(count)]
    if finish:
        states = [entries(tab_ref, ktab_ref, base + n, heads[n], (zero, zero)) for n in range(count)]

        def store(n, at, state):
            out_ref[n, 0, at, :] = state[0]
            out_ref[n, 1, at, :] = state[1]

        walk(length, count, units, states, keep_ref, load, store)
        for n in range(count):
            high, low = split(jnp.concatenate([out_ref[n, 0], out_ref[n, 1]], axis=1))
            turned = turned_ref[(base + n) * GROUP : (base + n + 1) * GROUP, :]
            grad_ref[n] = fold(matmul(turned, high) + matmul(turned, low))


def scan_both(base, count, place, rows, parts, high, low, tab, ktab, keep, turned):
    tokens = keep.shape[0]
    peers = len(parts) + 1
    out = [((count, 2, tokens, LANES), F32), ((2, count, LANES), F32), ((count, SIZE, GROUP), F32)]
    return call(functools.partial(scan_kernel, tokens // CHUNKS, base, count, peers, True, True, 0), out,
                (tab, ktab, keep, place, rows, high, low, *parts, turned), [VMEM] * 3 + [SMEM] + [VMEM] * (peers + 3),
                [pltpu.VMEM((tokens, count * GROUP), BF16), pltpu.VMEM((count, 2, tokens, LANES), F32)], count * 4 * 2 * 256**3)


def scan_first(base, count, place, rows, parts, high, low, tab, ktab, keep, ahead):
    tokens = keep.shape[0]
    peers = len(parts) + 1
    out = [((count, 2, tokens, LANES), F32), ((count, 2) + TILE, F32), ((2 * (base + count) + CHUNKS, LANES), F32)]
    return call(functools.partial(scan_kernel, tokens // CHUNKS, base, count, peers, True, False, len(ahead)), out,
                (tab, ktab, keep, place, rows, high, low, *parts, *ahead), [VMEM] * 3 + [SMEM] + [VMEM] * (peers + 2 + len(ahead)),
                [pltpu.VMEM((tokens, count * GROUP), BF16)], count * 2 * 2 * 256**3)


def scan_second(base, count, spaced, head, tab, ktab, keep, turned):
    tokens = keep.shape[0]
    out = [((count, 2, tokens, LANES), F32), ((count, SIZE, GROUP), F32)]
    return call(functools.partial(scan_kernel, tokens // CHUNKS, base, count, 0, False, True, 0), out,
                (tab, ktab, keep, turned, spaced, head), [VMEM] * 6, (), count * 2 * 2 * 256**3)


def merge_kernel(half, side_ref, entry_ref, weight_ref, *refs):
    parts, (own_ref, away_ref) = refs[:-2], refs[-2:]
    blocks = [part.at[n] for part in parts for n in range(part.shape[0])]
    side = side_ref[0]
    for n in range(half):
        for out_ref, which in ((own_ref, side), (away_ref, 1 - side)):
            here = jnp.where(which == 0, blocks[n][...], blocks[half + n][...])
            at = which * half + n
            re, im = entry_ref[0, pl.ds(at, 1), :], entry_ref[1, pl.ds(at, 1), :]
            weight = weight_ref[at]
            w_re, w_im = weight[:, :LANES], weight[:, LANES:]
            out_ref[n * SIZE : (n + 1) * SIZE, :LANES] = here[:, :LANES] + (re * w_re - im * w_im)
            out_ref[n * SIZE : (n + 1) * SIZE, LANES:] = here[:, LANES:] + (re * w_im + im * w_re)


def merge(half, side, entry, weight, parts):
    return call(functools.partial(merge_kernel, half), [((half * SIZE, GROUP), F32)] * 2,
                (side, entry, weight, *parts), [SMEM] + [VMEM] * (2 + len(parts)))


def state_kernel(base, sizes, entry_ref, decay_ref, high_ref, low_ref, *refs):
    parts, out_ref = refs[: len(sizes)], refs[-1]
    g = pl.program_id(0)
    re, im = entry_ref[0, pl.ds(base + g, 1), :], entry_ref[1, pl.ds(base + g, 1), :]
    d_re, d_im = decay_ref[0, 0], decay_ref[0, 1]
    z_re, z_im = parts[0][0, 0], parts[0][0, 1]
    if len(parts) > 1:
        first = g < sizes[0]
        z_re, z_im = jnp.where(first, z_re, parts[1][0, 0]), jnp.where(first, z_im, parts[1][0, 1])
    z_re = z_re + (re * d_re - im * d_im)
    z_im = z_im + (re * d_im + im * d_re)
    z_high, z_low = split(jnp.concatenate([z_re, z_im], axis=1))
    out = matmul(z_high, high_ref[0], NT) + matmul(z_high, low_ref[0], NT) + matmul(z_low, high_ref[0], NT)
    out_ref[...] = out.astype(BF16)


def states(base, parts, decay, entry, high, low, filled=None):
    groups = high.shape[0]
    tokens = parts[0].shape[2]
    sizes = [part.shape[0] for part in parts]
    each = lambda shape: pl.BlockSpec((1,) + shape, lambda g: (g + base, 0, 0, 0)[: len(shape) + 1])
    shape = (1, 2, tokens, LANES)
    picks = [pl.BlockSpec(shape, lambda g: (jnp.minimum(g, sizes[0] - 1), 0, 0, 0))]
    picks += [pl.BlockSpec(shape, lambda g: (jnp.maximum(g - sizes[0], 0), 0, 0, 0)) for _ in parts[1:]]
    args = [entry, decay, high, low, *parts]
    specs = [pl.BlockSpec(entry.shape, lambda g: (0, 0, 0)), each((2, tokens, LANES)), each((GROUP, GROUP)), each((GROUP, GROUP)), *picks]
    alias = {}
    if filled is not None:
        alias = {len(args): 0}
        args.append(filled)
        specs.append(pl.BlockSpec(memory_space=pl.ANY))
    return pl.pallas_call(
        functools.partial(state_kernel, base, sizes),
        grid=(sum(sizes),),
        in_specs=specs,
        out_specs=pl.BlockSpec((tokens, GROUP), lambda g: (0, g + base)),
        out_shape=jax.ShapeDtypeStruct((tokens, groups * GROUP), BF16),
        input_output_aliases=alias,
        name="states",
        compiler_params=pltpu.CompilerParams(vmem_limit_bytes=LIMIT),
        cost_estimate=pl.CostEstimate(flops=sum(sizes) * 3 * 2 * 256**3, bytes_accessed=sum(sizes) * 900_000, transcendentals=0),
    )(*args)


def final_kernel(flip, side_ref, x_ref, high_ref, low_ref, *refs):
    out_hbm, out_ref, sems = refs[-3:]
    half = high_ref.shape[0] // 2
    which = 1 - side_ref[0] if flip else side_ref[0]
    copies = []
    for n in range(half):
        at = which * half + n
        x = x_ref[n * SIZE : (n + 1) * SIZE, :]
        out = matmul(high_ref[at], x, NT) + matmul(low_ref[at], x, NT)
        for j in range(4):
            out_ref[4 * n + j] = out[j * SIZE : (j + 1) * SIZE]
        copies.append(pltpu.make_async_copy(out_ref.at[pl.ds(4 * n, 4)], out_hbm.at[pl.ds(at * 4, 4)], sems.at[n]))
        copies[-1].start()
    for copy in copies:
        copy.wait()


def final(flip, side, x, high, low, filled=None):
    half = high.shape[0] // 2
    blocks = high.shape[0] * 4
    args = [side, x, high, low]
    specs = [SMEM] + [VMEM] * 3
    alias = {}
    if filled is not None:
        alias = {len(args): 0}
        args.append(filled)
        specs.append(HBM)
    return pl.pallas_call(
        functools.partial(final_kernel, flip),
        out_shape=jax.ShapeDtypeStruct((blocks, SIZE, SIZE), F32),
        in_specs=specs,
        out_specs=HBM,
        scratch_shapes=[pltpu.VMEM((4 * half, SIZE, SIZE), F32), pltpu.SemaphoreType.DMA((half,))],
        input_output_aliases=alias,
        name="final",
        compiler_params=pltpu.CompilerParams(vmem_limit_bytes=LIMIT),
        cost_estimate=pl.CostEstimate(flops=half * 2 * 2 * 256 * 256 * 64, bytes_accessed=half * 400_000, transcendentals=0),
    )(*args)


def swap(x, axis, k):
    n = lax.axis_size(axis)
    return lax.ppermute(x, axis, [(i, i ^ k) for i in range(n)])


def entering(sent, far, axis, early_bits):
    peers = lax.axis_size(axis)
    rows = far[0].shape[0]
    first, total = (sent[:rows], sent[rows : 2 * rows]), sent[2 * rows : 2 * rows + 1]
    entry = (jnp.zeros_like(first[0]), jnp.zeros_like(first[1]))
    gap = (jnp.ones_like(first[0]), jnp.zeros_like(first[0]))
    k = 1
    for early in early_bits:
        if k > 1:
            sent = jnp.concatenate([first[0], first[1], jnp.broadcast_to(total, (8, LANES))])
        got = swap(sent, axis, k)
        other = (got[:rows], got[rows : 2 * rows])
        other_total = got[2 * rows : 2 * rows + 1]
        reach = times(gap, other)
        entry = tuple(jnp.where(early, e + r, e) for e, r in zip(entry, reach))
        if 2 * k < peers:
            step = times(gap, far)
            gap = tuple(jnp.where(early, other_total * s, g) for s, g in zip(step, gap))
            near = tuple(jnp.where(early, a, b) for a, b in zip(first, other))
            late = tuple(jnp.where(early, b, a) for a, b in zip(first, other))
            moved = times(far, late)
            first = tuple(a + jnp.where(early, total, other_total) * b for a, b in zip(near, moved))
            total = total * other_total
            far = times(far, far)
        k *= 2
    return jnp.stack(entry)


def exchanges(axes):
    steps = []
    for axis in axes:
        k = 1
        while k < lax.axis_size(axis):
            steps.append((axis, k))
            k *= 2
    return steps


def bits(steps):
    return [(lax.axis_index(axis).astype(jnp.uint32) // jnp.uint32(k)) & jnp.uint32(1) for axis, k in steps]


def piece(x, start, size):
    return lax.dynamic_slice(x, (start, jnp.uint32(0)), (size, x.shape[1]))


def total_sum(own, away, steps, starts):
    x = own + swap(away, *steps[0])
    for (axis, k), (here, there, _) in zip(steps[1:-1], starts):
        m = x.shape[0] // 2
        x = piece(x, here, m) + swap(piece(x, there, m), axis, k)
    x = (x + swap(x, *steps[-1])).astype(BF16)
    for (axis, k), (_, _, lower) in list(zip(steps[1:-1], starts))[::-1]:
        other = swap(x, axis, k)
        x = jnp.where(lower, jnp.concatenate([x, other]), jnp.concatenate([other, x]))
    return x


def inner(out_grad, prev_state, boundary, angle_code, radius_code, reflect):
    peers, place = lax.axis_size("tensor"), lax.axis_index("tensor")
    rows = out_grad[0]
    channels = prev_state.shape[2]
    tokens = prev_state.shape[1]
    groups = channels // GROUP
    half = groups // 2
    counts = [max(1, groups * 5 // 8)]
    counts.append(groups - counts[0])
    bases = [sum(counts[:n]) for n in range(len(counts))]
    place = place.astype(jnp.uint32)

    def away(k, base, count):
        start = (place ^ jnp.uint32(k)) * jnp.uint32(channels) + jnp.uint32(base * GROUP)
        return lax.dynamic_slice(rows, (jnp.uint32(0), start), (rows.shape[0], count * GROUP))

    parts = []
    for at in zip(bases, counts):
        parts.append([swap(away(k, *at), "tensor", k) for k in range(1, peers)])
    steps = exchanges(("dp", "ctx"))
    size = half * SIZE
    starts = []
    for bit in bits(steps)[1:-1]:
        size //= 2
        starts.append((bit * jnp.uint32(size), (jnp.uint32(1) - bit) * jnp.uint32(size), bit == 0))
    side = jnp.reshape(lax.axis_index("dp") & 1, (1,))
    place = jnp.reshape(place.astype(jnp.int32), (1,))
    early = [bit == 0 for bit in bits(exchanges(("ctx",)))]
    code = angle_code * 1024 + radius_code
    code, side, place, starts, early = lax.optimization_barrier((code, side, place, starts, early))
    high, low, tab, far = basis(code, reflect, tokens // CHUNKS)
    keep, ktab, turned, decay, weight = weights(boundary, tab, prev_state[0])
    done = []
    for base, count, part in zip(bases[:-1], counts[:-1], parts[:-1]):
        done.append(scan_both(base, count, place, rows, part, high, low, tab, ktab, keep, turned))
    base, count = bases[-1], counts[-1]
    spaced, head, sent = scan_first(base, count, place, rows, parts[-1], high, low, tab, ktab, keep, [d[1] for d in done])
    entry = entering(sent, (far[0], far[1]), "ctx", early)
    z_last, grad_last = scan_second(base, count, spaced, head, tab, ktab, keep, turned)
    own, other = merge(half, side, entry, weight, [d[2] for d in done] + [grad_last])
    z = [d[0] for d in done] + [z_last]
    grad_input = states(0, z[:1], decay, entry, high, low)
    grad_input = states(bases[1], z[1:], decay, entry, high, low, grad_input)
    own = total_sum(own, other, steps, starts)
    other = swap(own, *steps[0])
    grad_transition = final(False, side, own, high, low)
    grad_transition = final(True, side, other, high, low, grad_transition)
    return grad_input[None], grad_transition


def solution(mesh):
    in_specs = (
        P("dp", ("ctx", "tensor"), None),
        P("dp", "ctx", "tensor"),
        P("dp", "ctx"),
        P("tensor", None),
        P("tensor", None),
        P("tensor", None, None),
    )
    out_specs = (P("dp", "ctx", "tensor"), P("tensor", None, None))
    return jax.shard_map(inner, mesh=mesh, in_specs=in_specs, out_specs=out_specs, check_vma=False)
```

```python
import functools
import math

import jax
import jax.numpy as jnp
from jax import lax
from jax.experimental import pallas as pl
from jax.experimental.pallas import tpu as pltpu
from jax.sharding import PartitionSpec as P


F32 = jnp.float32
BF16 = jnp.bfloat16
LANES = 128
CHUNKS = 8
GROUP = 256
SIZE = 64
TILE = (CHUNKS, LANES)
LIMIT = 16 << 20
NN = ((1,), (0,))
NT = ((1,), (1,))
TN = ((0,), (0,))


def iota(shape, dim):
    return lax.broadcasted_iota(jnp.int32, shape, dim)


def matmul(a, b, dims=NN, precision=None):
    return lax.dot_general(a, b, (dims, ((), ())), precision=precision, preferred_element_type=F32)


def split(x):
    high = x.astype(BF16)
    return high, (x - high.astype(F32)).astype(BF16)


def split3(x):
    high = x.astype(BF16)
    rest = x - high.astype(F32)
    middle = rest.astype(BF16)
    return high, middle, (rest - middle.astype(F32)).astype(BF16)


def times(a, b):
    return a[0] * b[0] - a[1] * b[1], a[0] * b[1] + a[1] * b[0]


def later(x, k, fill):
    return jnp.where(iota(TILE, 0) < CHUNKS - k, pltpu.roll(x, CHUNKS - k, 0), fill)


def earlier(x, k, fill):
    return jnp.where(iota(TILE, 0) >= k, pltpu.roll(x, k, 0), fill)


def power(tab_ref, g, n):
    return tuple(jnp.broadcast_to(tab_ref[g, c, n : n + 1], TILE) for c in range(2))


def entries(tab_ref, ktab_ref, g, head, entry):
    last = iota(TILE, 0) == CHUNKS - 1
    moved = times(power(tab_ref, g, 1), entry)
    scan = tuple(jnp.where(last, ktab_ref[0] * m, 0.0) for m in moved)
    if head is not None:
        scan = tuple(h + s for h, s in zip(head, scan))
    for n in range(3):
        near = tuple(later(x, 1 << n, 0.0) for x in scan)
        moved = times(power(tab_ref, g, 1 << n), near)
        scan = tuple(s + ktab_ref[n] * m for s, m in zip(scan, moved))
    return tuple(jnp.where(last, e, pltpu.roll(s, CHUNKS - 1, 0)) for e, s in zip(entry, scan))


def fold(x):
    block = (iota((SIZE, GROUP), 1) % LANES) // 32
    out = x[:SIZE]
    for j in range(1, 4):
        out = jnp.where(block == j, x[j * SIZE : (j + 1) * SIZE], out)
    return out


def walk(length, groups, units, states, keep_ref, load, store):
    for i in range(length - 1, -1, -1):
        at = pl.ds(i, CHUNKS, stride=length)
        keep = keep_ref[at, :]
        for n in range(groups):
            re, im = states[n]
            step_re, step_im = keep * units[n][0], keep * units[n][1]
            if load is None:
                states[n] = (step_re * re - step_im * im, step_re * im + step_im * re)
            else:
                a, b = load(n, at)
                states[n] = ((a + step_re * re) - step_im * im, (b + step_re * im) + step_im * re)
            if store is not None:
                store(n, at, states[n])
    return states


def basis_kernel(length, code_ref, reflect_ref, high_ref, low_ref, tab_ref, far_ref, u_ref, wide_ref):
    rows = reflect_ref.shape[0]
    blocks = rows // 4
    groups = blocks // 4

    wide_ref[...] = jnp.concatenate([code_ref[...]] * 4, axis=1)
    codes = wide_ref[pl.ds(0, groups, stride=4), :]
    block = iota(codes.shape, 1) // 32
    for j in range(1, 4):
        codes = jnp.where(block == j, wide_ref[pl.ds(j, groups, stride=4), :], codes)

    rates = jnp.exp(-math.log(2.0) * (4.0 + (codes & 1023).astype(F32) * (10.0 / 1024.0)))
    series = jnp.full_like(rates, 1.0 / 8.0)
    for k in range(7, 0, -1):
        series = series * rates + 1.0 / k
    logs = -rates * series
    angles = codes >> 10
    row = iota(TILE, 0)
    n = jnp.where(row == 0, 1, row * length)
    for g in range(groups):
        turn = ((n * angles[g : g + 1, :]) & 8191).astype(F32) * (math.pi / 4096.0)
        size = jnp.exp(n.astype(F32) * logs[g : g + 1, :])
        re, im = size * jnp.cos(turn), -size * jnp.sin(turn)
        tab_ref[g, 0] = re
        tab_ref[g, 1] = im
        half = (re[4:5], im[4:5])
        whole = times(half, half)
        far_ref[0, g : g + 1, :] = whole[0]
        far_ref[1, g : g + 1, :] = whole[1]

    v = [reflect_ref[pl.ds(k, blocks, stride=4), :] for k in range(4)]
    u = []
    for k in range(4):
        now = v[k]
        for l in range(k):
            now = now - u[l] * jnp.sum(v[l] * v[k], axis=1, keepdims=True)
        u.append(now * (2.0 / jnp.sum(v[k] * v[k], axis=1, keepdims=True)))
        u_ref[pl.ds(k, blocks, stride=4), :] = u[k]
    to = iota((SIZE, SIZE), 1)
    sort = jnp.where(iota((SIZE, SIZE), 0) == (to % 32) * 2 + to // 32, 1.0, 0.0).astype(F32)
    sorted_v = matmul(reflect_ref[...], sort, NN, lax.Precision.HIGHEST)
    wide = (rows, GROUP)
    block = (iota(wide, 0) // 4) % 4
    wide_v = jnp.concatenate([sorted_v[:, :32]] * 4 + [sorted_v[:, 32:]] * 4, axis=1)
    wide_v = split3(jnp.where(block == (iota(wide, 1) % LANES) // 32, wide_v, 0.0))
    wide_u = split3(jnp.where(block == iota(wide, 1) // SIZE, jnp.concatenate([u_ref[...]] * 4, axis=1), 0.0))
    to = iota((GROUP, GROUP), 1)
    order = jnp.where(iota((GROUP, GROUP), 0) == ((to % LANES) // 32) * SIZE + (to % 32) * 2 + to // LANES, 1.0, 0.0).astype(F32)
    for g in range(groups):
        at = slice(g * 16, (g + 1) * 16)
        left = jnp.concatenate([wide_u[n][at] for n in (0, 0, 1, 0, 1, 2)], axis=0)
        right = jnp.concatenate([wide_v[n][at] for n in (0, 1, 0, 2, 1, 0)], axis=0)
        high, low = split(order - matmul(left, right, TN))
        high_ref[g] = high
        low_ref[g] = low


def weight_kernel(length, boundary_ref, tab_ref, prev_ref, keep_ref, ktab_ref, turned_ref, decay_ref, weight_ref):
    groups = tab_ref.shape[0]
    keep = jnp.where(boundary_ref[...] == 1, 0.6, 1.0).astype(F32)
    keep_ref[...] = jnp.broadcast_to(keep, (LANES, keep.shape[1])).T

    chunk = keep_ref[pl.ds(0, CHUNKS, stride=length), :]
    for i in range(1, length):
        chunk = chunk * keep_ref[pl.ds(i, CHUNKS, stride=length), :]
    two = chunk * later(chunk, 1, 1.0)
    four = two * later(two, 2, 1.0)
    before = earlier(chunk, 1, 1.0)
    before = before * earlier(before, 1, 1.0)
    before = before * earlier(before, 2, 1.0)
    before = before * earlier(before, 4, 1.0)
    eight = four * later(four, 4, 1.0)
    ktab_ref[0] = chunk
    ktab_ref[1] = two
    ktab_ref[2] = four
    ktab_ref[3] = before
    ktab_ref[4] = jnp.broadcast_to(eight[0:1], TILE)

    one, zero = jnp.ones(TILE, F32), jnp.zeros(TILE, F32)
    for first in range(0, groups, 4):
        some = range(first, min(first + 4, groups))
        states = [entries(tab_ref, ktab_ref, g, None, (one, zero)) for g in some]
        units = [power(tab_ref, g, 0) for g in some]

        def store(k, at, state):
            decay_ref[first + k, 0, at, :] = state[0]
            decay_ref[first + k, 1, at, :] = state[1]

        walk(length, len(some), units, states, keep_ref, None, store)
    for g in range(groups):
        columns = slice(g * GROUP, (g + 1) * GROUP)
        turned = prev_ref[:, columns].T
        turned_ref[columns, :] = turned
        high, low = split(jnp.concatenate([decay_ref[g, 0], decay_ref[g, 1]], axis=1))
        weight_ref[g] = fold(matmul(turned, high) + matmul(turned, low))


VMEM = pl.BlockSpec(memory_space=pltpu.VMEM)
SMEM = pl.BlockSpec(memory_space=pltpu.SMEM)
HBM = pl.BlockSpec(memory_space=pltpu.HBM)


def call(kernel, out_shape, args, specs, scratch=(), flops=0):
    shapes = [jax.ShapeDtypeStruct(s, t) for s, t in out_shape]
    moved = sum(a.size * a.dtype.itemsize for a in args) + sum(s.size * s.dtype.itemsize for s in shapes)
    return pl.pallas_call(
        kernel,
        out_shape=shapes,
        in_specs=specs,
        out_specs=[VMEM] * len(shapes),
        scratch_shapes=list(scratch),
        compiler_params=pltpu.CompilerParams(vmem_limit_bytes=LIMIT),
        cost_estimate=pl.CostEstimate(flops=int(flops), bytes_accessed=int(moved), transcendentals=0),
    )(*args)


def basis(code, reflect, length):
    blocks = reflect.shape[0]
    groups = blocks // 4
    out = [
        ((groups, GROUP, GROUP), BF16),
        ((groups, GROUP, GROUP), BF16),
        ((groups, 2) + TILE, F32),
        ((2, groups, LANES), F32),
    ]
    args = (code, reflect.reshape(blocks * 4, SIZE))
    scratch = [pltpu.VMEM((blocks * 4, SIZE), F32), pltpu.VMEM((blocks, LANES), jnp.int32)]
    return call(functools.partial(basis_kernel, length), out, args, [VMEM] * 2, scratch, groups * 2 * 2 * 256**3)


def weights(boundary, tab, prev):
    groups = tab.shape[0]
    tokens, channels = prev.shape
    out = [
        ((tokens, LANES), F32),
        ((5,) + TILE, F32),
        ((channels, tokens), BF16),
        ((groups, 2, tokens, LANES), F32),
        ((groups, SIZE, GROUP), F32),
    ]
    return call(functools.partial(weight_kernel, tokens // CHUNKS), out, (boundary, tab, prev), [VMEM] * 3, (), groups * 2 * 2 * 256**3)


def scan_kernel(length, base, count, peers, begin, finish, aheads, *refs):
    refs = list(refs)
    take = lambda n: [refs.pop(0) for _ in range(n)]
    tab_ref, ktab_ref, keep_ref = take(3)
    if begin:
        place_ref, own_ref, high_ref, low_ref = take(4)
        others = take(peers - 1)
    if begin and not finish:
        ahead = take(aheads)
    if finish:
        (turned_ref,) = take(1)
    if begin:
        out_ref, head_ref, first_ref = take(3) if not finish else take(1) + [None] + take(1)
    else:
        in_ref, head_ref, out_ref = take(3)
    if finish:
        (grad_ref,) = take(1)
    heads = []
    if begin:
        rows_ref, = take(1)
        spaced_ref = take(1)[0] if finish else out_ref
        size = own_ref.shape[0]
        width = count * GROUP
        place = place_ref[0]
        channels = high_ref.shape[0] * GROUP
        at = pl.ds(pl.multiple_of(place * size, size), size)
        rows_ref[at, :] = own_ref[:, pl.ds(pl.multiple_of(place * channels + base * GROUP, GROUP), width)]
        for k in range(1, peers):
            rows_ref[pl.ds(pl.multiple_of((place ^ k) * size, size), size), :] = others[k - 1][...]
        for n in range(count):
            rows = rows_ref[:, n * GROUP : (n + 1) * GROUP]
            out = matmul(rows, high_ref[base + n]) + matmul(rows, low_ref[base + n])
            spaced_ref[n, 0] = out[:, :LANES]
            spaced_ref[n, 1] = out[:, LANES:]
    else:
        spaced_ref = in_ref
    load = lambda n, at: (spaced_ref[n, 0, at, :], spaced_ref[n, 1, at, :])
    units = [power(tab_ref, base + n, 0) for n in range(count)]
    zero = jnp.zeros(TILE, F32)
    if begin and not finish:
        groups = base + count
        at = 0
        for ref in ahead:
            size = ref.shape[1]
            for c in range(2):
                first_ref[c * groups + at : c * groups + at + size, :] = ref[c]
            at += size
        first_ref[2 * groups :, :] = ktab_ref[4]
    if begin:
        heads = walk(length, count, units, [(zero, zero)] * count, keep_ref, load, None)
        before = ktab_ref[3]
        for n in range(count):
            if head_ref is not None:
                head_ref[n, 0] = heads[n][0]
                head_ref[n, 1] = heads[n][1]
            hop = tuple(jnp.where(iota(TILE, 0) == 0, one, tab_ref[base + n, c]) for c, one in ((0, 1.0), (1, 0.0)))
            moved = times(hop, heads[n])
            for c in range(2):
                value = jnp.sum(moved[c] * before, axis=0, keepdims=True)
                if finish:
                    first_ref[c, n : n + 1, :] = value
                else:
                    first_ref[c * groups + base + n : c * groups + base + n + 1, :] = value
    else:
        heads = [(head_ref[n, 0], head_ref[n, 1]) for n in range(count)]
    if finish:
        states = [entries(tab_ref, ktab_ref, base + n, heads[n], (zero, zero)) for n in range(count)]

        def store(n, at, state):
            out_ref[n, 0, at, :] = state[0]
            out_ref[n, 1, at, :] = state[1]

        walk(length, count, units, states, keep_ref, load, store)
        for n in range(count):
            high, low = split(jnp.concatenate([out_ref[n, 0], out_ref[n, 1]], axis=1))
            turned = turned_ref[(base + n) * GROUP : (base + n + 1) * GROUP, :]
            grad_ref[n] = fold(matmul(turned, high) + matmul(turned, low))


def scan_both(base, count, place, rows, parts, high, low, tab, ktab, keep, turned):
    tokens = keep.shape[0]
    peers = len(parts) + 1
    out = [((count, 2, tokens, LANES), F32), ((2, count, LANES), F32), ((count, SIZE, GROUP), F32)]
    return call(functools.partial(scan_kernel, tokens // CHUNKS, base, count, peers, True, True, 0), out,
                (tab, ktab, keep, place, rows, high, low, *parts, turned), [VMEM] * 3 + [SMEM] + [VMEM] * (peers + 3),
                [pltpu.VMEM((tokens, count * GROUP), BF16), pltpu.VMEM((count, 2, tokens, LANES), F32)], count * 4 * 2 * 256**3)


def scan_first(base, count, place, rows, parts, high, low, tab, ktab, keep, ahead):
    tokens = keep.shape[0]
    peers = len(parts) + 1
    out = [((count, 2, tokens, LANES), F32), ((count, 2) + TILE, F32), ((2 * (base + count) + CHUNKS, LANES), F32)]
    return call(functools.partial(scan_kernel, tokens // CHUNKS, base, count, peers, True, False, len(ahead)), out,
                (tab, ktab, keep, place, rows, high, low, *parts, *ahead), [VMEM] * 3 + [SMEM] + [VMEM] * (peers + 2 + len(ahead)),
                [pltpu.VMEM((tokens, count * GROUP), BF16)], count * 2 * 2 * 256**3)


def scan_second(base, count, spaced, head, tab, ktab, keep, turned):
    tokens = keep.shape[0]
    out = [((count, 2, tokens, LANES), F32), ((count, SIZE, GROUP), F32)]
    return call(functools.partial(scan_kernel, tokens // CHUNKS, base, count, 0, False, True, 0), out,
                (tab, ktab, keep, turned, spaced, head), [VMEM] * 6, (), count * 2 * 2 * 256**3)


def merge_kernel(half, side_ref, entry_ref, weight_ref, *refs):
    parts, (own_ref, away_ref) = refs[:-2], refs[-2:]
    blocks = [part.at[n] for part in parts for n in range(part.shape[0])]
    side = side_ref[0]
    for n in range(half):
        for out_ref, which in ((own_ref, side), (away_ref, 1 - side)):
            here = jnp.where(which == 0, blocks[n][...], blocks[half + n][...])
            at = which * half + n
            re, im = entry_ref[0, pl.ds(at, 1), :], entry_ref[1, pl.ds(at, 1), :]
            weight = weight_ref[at]
            w_re, w_im = weight[:, :LANES], weight[:, LANES:]
            out_ref[n * SIZE : (n + 1) * SIZE, :LANES] = here[:, :LANES] + (re * w_re - im * w_im)
            out_ref[n * SIZE : (n + 1) * SIZE, LANES:] = here[:, LANES:] + (re * w_im + im * w_re)


def merge(half, side, entry, weight, parts):
    return call(functools.partial(merge_kernel, half), [((half * SIZE, GROUP), F32)] * 2,
                (side, entry, weight, *parts), [SMEM] + [VMEM] * (2 + len(parts)))


def state_kernel(base, sizes, entry_ref, decay_ref, high_ref, low_ref, *refs):
    parts, out_ref = refs[: len(sizes)], refs[-1]
    g = pl.program_id(0) + base
    re, im = entry_ref[0, pl.ds(g, 1), :], entry_ref[1, pl.ds(g, 1), :]
    d_re, d_im = decay_ref[0, 0], decay_ref[0, 1]
    z_re, z_im = parts[0][0, 0], parts[0][0, 1]
    start = 0
    for size, part in zip(sizes[:-1], parts[1:]):
        start += size
        z_re, z_im = jnp.where(g < start, z_re, part[0, 0]), jnp.where(g < start, z_im, part[0, 1])
    z_re = z_re + (re * d_re - im * d_im)
    z_im = z_im + (re * d_im + im * d_re)
    z_high, z_low = split(jnp.concatenate([z_re, z_im], axis=1))
    out = matmul(z_high, high_ref[0], NT) + matmul(z_high, low_ref[0], NT) + matmul(z_low, high_ref[0], NT)
    out_ref[...] = out.astype(BF16)


def states(base, count, parts, decay, entry, high, low, filled=None):
    groups = high.shape[0]
    tokens = parts[0].shape[2]
    sizes = [part.shape[0] for part in parts]
    each = lambda shape: pl.BlockSpec((1,) + shape, lambda g: (g + base, 0, 0, 0)[: len(shape) + 1])

    def pick(start, size):
        return pl.BlockSpec((1, 2, tokens, LANES), lambda g: (jnp.minimum(jnp.maximum(g + base - start, 0), size - 1), 0, 0, 0))

    args = [entry, decay, high, low, *parts]
    specs = [pl.BlockSpec(entry.shape, lambda g: (0, 0, 0)), each((2, tokens, LANES)), each((GROUP, GROUP)), each((GROUP, GROUP))]
    specs += [pick(sum(sizes[:n]), size) for n, size in enumerate(sizes)]
    alias = {}
    if filled is not None:
        alias = {len(args): 0}
        args.append(filled)
        specs.append(pl.BlockSpec(memory_space=pl.ANY))
    return pl.pallas_call(
        functools.partial(state_kernel, base, sizes),
        grid=(count,),
        in_specs=specs,
        out_specs=pl.BlockSpec((tokens, GROUP), lambda g: (0, g + base)),
        out_shape=jax.ShapeDtypeStruct((tokens, groups * GROUP), BF16),
        input_output_aliases=alias,
        name="states",
        compiler_params=pltpu.CompilerParams(vmem_limit_bytes=LIMIT),
        cost_estimate=pl.CostEstimate(flops=count * 3 * 2 * 256**3, bytes_accessed=count * 900_000, transcendentals=0),
    )(*args)


EXTRA = 16
STEPS = 32000.0


def encode(x, code_ref):
    rows = x.shape[0]
    most = jnp.maximum(jnp.max(jnp.abs(x), axis=0, keepdims=True), 1e-30)
    power = jnp.ceil(jnp.log2(most))
    code = jnp.floor(x * (jnp.exp2(-power) * STEPS) + 0.5)
    code_ref[:rows, :] = code.astype(jnp.int32).astype(jnp.int16)
    code_ref[rows:, :] = jnp.broadcast_to(power, (EXTRA, power.shape[1])).astype(jnp.int32).astype(jnp.int16)


def decode(code_ref, start=0, rows=None):
    if rows is None:
        rows = code_ref.shape[0] - EXTRA
    power = code_ref[start + rows : start + rows + EXTRA, :].astype(jnp.int32).astype(F32)[:1]
    return code_ref[start : start + rows, :].astype(jnp.int32).astype(F32) * (jnp.exp2(power) * (1.0 / STEPS))


def halve_kernel(bit_ref, own_ref, got_ref, here_ref, code_ref):
    rows = here_ref.shape[0]
    bit = bit_ref[0]
    here, there = (pl.ds(pl.multiple_of(n * rows, rows), rows) for n in (bit, 1 - bit))
    here_ref[...] = own_ref[here, :] + got_ref[here, :]
    encode(own_ref[there, :] + got_ref[there, :], code_ref)


def halve(bit, own, got):
    rows, width = own.shape[0] // 2, own.shape[1]
    out = [((rows, width), F32), ((rows + EXTRA, width), jnp.dtype(jnp.int16))]
    return call(halve_kernel, out, (bit, own, got), [SMEM, VMEM, VMEM])


def add_kernel(own_ref, got_ref, code_ref):
    own = own_ref[...] if own_ref.dtype == F32 else decode(own_ref)
    encode(own + decode(got_ref), code_ref)


def add(own, got):
    return call(add_kernel, [(got.shape, got.dtype)], (own, got), [VMEM, VMEM])[0]


def final_kernel(flip, side_ref, x_ref, high_ref, low_ref, *refs):
    out_hbm, out_ref, sems = refs[-3:]
    half = high_ref.shape[0] // 2
    which = 1 - side_ref[0] if flip else side_ref[0]
    copies = []
    rows = x_ref.shape[0] // 2 - EXTRA
    x = jnp.concatenate([decode(x_ref, n * (rows + EXTRA), rows) for n in range(2)], axis=0)
    for n in range(half):
        at = which * half + n
        x_high, x_low = split(x[n * SIZE : (n + 1) * SIZE, :])
        out = matmul(high_ref[at], x_high, NT) + matmul(low_ref[at], x_high, NT) + matmul(high_ref[at], x_low, NT)
        for j in range(4):
            out_ref[4 * n + j] = out[j * SIZE : (j + 1) * SIZE]
        copies.append(pltpu.make_async_copy(out_ref.at[pl.ds(4 * n, 4)], out_hbm.at[pl.ds(at * 4, 4)], sems.at[n]))
        copies[-1].start()
    for copy in copies:
        copy.wait()


def final(flip, side, x, high, low, filled=None):
    half = high.shape[0] // 2
    blocks = high.shape[0] * 4
    args = [side, x, high, low]
    specs = [SMEM] + [VMEM] * 3
    alias = {}
    if filled is not None:
        alias = {len(args): 0}
        args.append(filled)
        specs.append(HBM)
    return pl.pallas_call(
        functools.partial(final_kernel, flip),
        out_shape=jax.ShapeDtypeStruct((blocks, SIZE, SIZE), F32),
        in_specs=specs,
        out_specs=HBM,
        scratch_shapes=[pltpu.VMEM((4 * half, SIZE, SIZE), F32), pltpu.SemaphoreType.DMA((half,))],
        input_output_aliases=alias,
        name="final",
        compiler_params=pltpu.CompilerParams(vmem_limit_bytes=LIMIT),
        cost_estimate=pl.CostEstimate(flops=half * 3 * 2 * 256 * 256 * 64, bytes_accessed=half * 400_000, transcendentals=0),
    )(*args)


def swap(x, axis, k):
    n = lax.axis_size(axis)
    return lax.ppermute(x, axis, [(i, i ^ k) for i in range(n)])


def entering(sent, far, axis, early_bits):
    peers = lax.axis_size(axis)
    rows = far[0].shape[0]
    first, total = (sent[:rows], sent[rows : 2 * rows]), sent[2 * rows : 2 * rows + 1]
    entry = (jnp.zeros_like(first[0]), jnp.zeros_like(first[1]))
    gap = (jnp.ones_like(first[0]), jnp.zeros_like(first[0]))
    k = 1
    for early in early_bits:
        if k > 1:
            sent = jnp.concatenate([first[0], first[1], jnp.broadcast_to(total, (8, LANES))])
        got = swap(sent, axis, k)
        other = (got[:rows], got[rows : 2 * rows])
        other_total = got[2 * rows : 2 * rows + 1]
        reach = times(gap, other)
        entry = tuple(jnp.where(early, e + r, e) for e, r in zip(entry, reach))
        if 2 * k < peers:
            step = times(gap, far)
            gap = tuple(jnp.where(early, other_total * s, g) for s, g in zip(step, gap))
            near = tuple(jnp.where(early, a, b) for a, b in zip(first, other))
            late = tuple(jnp.where(early, b, a) for a, b in zip(first, other))
            moved = times(far, late)
            first = tuple(a + jnp.where(early, total, other_total) * b for a, b in zip(near, moved))
            total = total * other_total
            far = times(far, far)
        k *= 2
    return jnp.stack(entry)


def exchanges(axes):
    steps = []
    for axis in axes:
        k = 1
        while k < lax.axis_size(axis):
            steps.append((axis, k))
            k *= 2
    return steps


def bits(steps):
    return [(lax.axis_index(axis).astype(jnp.uint32) // jnp.uint32(k)) & jnp.uint32(1) for axis, k in steps]


def total_sum(own, away, steps, bit, lower):
    got = swap(away, *steps[0])
    here, code = halve(bit, own, got)
    got = swap(code, *steps[1])
    code = add(here, got)
    for step in steps[2:]:
        got = swap(code, *step)
        code = add(code, got)
    other = swap(code, *steps[1])
    return jnp.where(lower, jnp.concatenate([code, other]), jnp.concatenate([other, code]))


def inner(out_grad, prev_state, boundary, angle_code, radius_code, reflect):
    peers, place = lax.axis_size("tensor"), lax.axis_index("tensor")
    rows = out_grad[0]
    channels = prev_state.shape[2]
    tokens = prev_state.shape[1]
    groups = channels // GROUP
    half = groups // 2
    counts = [max(1, groups * 5 // 8)]
    counts.append(groups - counts[0])
    bases = [sum(counts[:n]) for n in range(len(counts))]
    place = place.astype(jnp.uint32)

    def away(k, base, count):
        start = (place ^ jnp.uint32(k)) * jnp.uint32(channels) + jnp.uint32(base * GROUP)
        return lax.dynamic_slice(rows, (jnp.uint32(0), start), (rows.shape[0], count * GROUP))

    parts = []
    for at in zip(bases, counts):
        parts.append([swap(away(k, *at), "tensor", k) for k in range(1, peers)])
    steps = exchanges(("dp", "ctx"))
    bit = bits(steps)[1]
    lower = bit == 0
    bit = jnp.reshape(bit.astype(jnp.int32), (1,))
    side = jnp.reshape(lax.axis_index("dp") & 1, (1,))
    place = jnp.reshape(place.astype(jnp.int32), (1,))
    early = [bit == 0 for bit in bits(exchanges(("ctx",)))]
    code = angle_code * 1024 + radius_code
    code, side, place, bit, lower, early = lax.optimization_barrier((code, side, place, bit, lower, early))
    high, low, tab, far = basis(code, reflect, tokens // CHUNKS)
    keep, ktab, turned, decay, weight = weights(boundary, tab, prev_state[0])
    done = []
    for base, count, part in zip(bases[:-1], counts[:-1], parts[:-1]):
        done.append(scan_both(base, count, place, rows, part, high, low, tab, ktab, keep, turned))
    base, count = bases[-1], counts[-1]
    spaced, head, sent = scan_first(base, count, place, rows, parts[-1], high, low, tab, ktab, keep, [d[1] for d in done])
    entry = entering(sent, (far[0], far[1]), "ctx", early)
    z_last, grad_last = scan_second(base, count, spaced, head, tab, ktab, keep, turned)
    own, other = merge(half, side, entry, weight, [d[2] for d in done] + [grad_last])
    z = [d[0] for d in done] + [z_last]
    grad_input = states(0, half, z, decay, entry, high, low)
    grad_input = states(half, groups - half, z, decay, entry, high, low, grad_input)
    own = total_sum(own, other, steps, bit, lower)
    other = swap(own, *steps[0])
    grad_transition = final(False, side, own, high, low)
    grad_transition = final(True, side, other, high, low, grad_transition)
    return grad_input[None], grad_transition


def solution(mesh):
    in_specs = (
        P("dp", ("ctx", "tensor"), None),
        P("dp", "ctx", "tensor"),
        P("dp", "ctx"),
        P("tensor", None),
        P("tensor", None),
        P("tensor", None, None),
    )
    out_specs = (P("dp", "ctx", "tensor"), P("tensor", None, None))
    return jax.shard_map(inner, mesh=mesh, in_specs=in_specs, out_specs=out_specs, check_vma=False)
```

```python
import functools
import math

import jax
import jax.numpy as jnp
from jax import lax
from jax.experimental import pallas as pl
from jax.experimental.pallas import tpu as pltpu
from jax.sharding import PartitionSpec as P


F32 = jnp.float32
BF16 = jnp.bfloat16
LANES = 128
CHUNKS = 8
GROUP = 256
SIZE = 64
TILE = (CHUNKS, LANES)
LIMIT = 16 << 20
NN = ((1,), (0,))
NT = ((1,), (1,))
TN = ((0,), (0,))


def iota(shape, dim):
    return lax.broadcasted_iota(jnp.int32, shape, dim)


def matmul(a, b, dims=NN, precision=None):
    return lax.dot_general(a, b, (dims, ((), ())), precision=precision, preferred_element_type=F32)


def split(x):
    high = x.astype(BF16)
    return high, (x - high.astype(F32)).astype(BF16)


def split3(x):
    high = x.astype(BF16)
    rest = x - high.astype(F32)
    middle = rest.astype(BF16)
    return high, middle, (rest - middle.astype(F32)).astype(BF16)


def times(a, b):
    return a[0] * b[0] - a[1] * b[1], a[0] * b[1] + a[1] * b[0]


def later(x, k, fill):
    return jnp.where(iota(TILE, 0) < CHUNKS - k, pltpu.roll(x, CHUNKS - k, 0), fill)


def earlier(x, k, fill):
    return jnp.where(iota(TILE, 0) >= k, pltpu.roll(x, k, 0), fill)


def power(tab_ref, g, n):
    return tuple(jnp.broadcast_to(tab_ref[g, c, n : n + 1], TILE) for c in range(2))


def entries(tab_ref, ktab_ref, g, head, entry):
    last = iota(TILE, 0) == CHUNKS - 1
    moved = times(power(tab_ref, g, 1), entry)
    scan = tuple(jnp.where(last, ktab_ref[0] * m, 0.0) for m in moved)
    if head is not None:
        scan = tuple(h + s for h, s in zip(head, scan))
    for n in range(3):
        near = tuple(later(x, 1 << n, 0.0) for x in scan)
        moved = times(power(tab_ref, g, 1 << n), near)
        scan = tuple(s + ktab_ref[n] * m for s, m in zip(scan, moved))
    return tuple(jnp.where(last, e, pltpu.roll(s, CHUNKS - 1, 0)) for e, s in zip(entry, scan))


def fold(x):
    block = (iota((SIZE, GROUP), 1) % LANES) // 32
    out = x[:SIZE]
    for j in range(1, 4):
        out = jnp.where(block == j, x[j * SIZE : (j + 1) * SIZE], out)
    return out


def walk(length, groups, units, states, keep_ref, load, store):
    for i in range(length - 1, -1, -1):
        at = pl.ds(i, CHUNKS, stride=length)
        keep = keep_ref[at, :]
        for n in range(groups):
            re, im = states[n]
            step_re, step_im = keep * units[n][0], keep * units[n][1]
            if load is None:
                states[n] = (step_re * re - step_im * im, step_re * im + step_im * re)
            else:
                a, b = load(n, at)
                states[n] = ((a + step_re * re) - step_im * im, (b + step_re * im) + step_im * re)
            if store is not None:
                store(n, at, states[n])
    return states


def basis_kernel(length, code_ref, reflect_ref, high_ref, low_ref, tab_ref, far_ref, u_ref, wide_ref):
    rows = reflect_ref.shape[0]
    blocks = rows // 4
    groups = blocks // 4

    wide_ref[...] = jnp.concatenate([code_ref[...]] * 4, axis=1)
    codes = wide_ref[pl.ds(0, groups, stride=4), :]
    block = iota(codes.shape, 1) // 32
    for j in range(1, 4):
        codes = jnp.where(block == j, wide_ref[pl.ds(j, groups, stride=4), :], codes)

    rates = jnp.exp(-math.log(2.0) * (4.0 + (codes & 1023).astype(F32) * (10.0 / 1024.0)))
    series = jnp.full_like(rates, 1.0 / 8.0)
    for k in range(7, 0, -1):
        series = series * rates + 1.0 / k
    logs = -rates * series
    angles = codes >> 10
    row = iota(TILE, 0)
    n = jnp.where(row == 0, 1, row * length)
    for g in range(groups):
        turn = ((n * angles[g : g + 1, :]) & 8191).astype(F32) * (math.pi / 4096.0)
        size = jnp.exp(n.astype(F32) * logs[g : g + 1, :])
        re, im = size * jnp.cos(turn), -size * jnp.sin(turn)
        tab_ref[g, 0] = re
        tab_ref[g, 1] = im
        half = (re[4:5], im[4:5])
        whole = times(half, half)
        far_ref[0, g : g + 1, :] = whole[0]
        far_ref[1, g : g + 1, :] = whole[1]

    v = [reflect_ref[pl.ds(k, blocks, stride=4), :] for k in range(4)]
    u = []
    for k in range(4):
        now = v[k]
        for l in range(k):
            now = now - u[l] * jnp.sum(v[l] * v[k], axis=1, keepdims=True)
        u.append(now * (2.0 / jnp.sum(v[k] * v[k], axis=1, keepdims=True)))
        u_ref[pl.ds(k, blocks, stride=4), :] = u[k]
    to = iota((SIZE, SIZE), 1)
    sort = jnp.where(iota((SIZE, SIZE), 0) == (to % 32) * 2 + to // 32, 1.0, 0.0).astype(F32)
    sorted_v = matmul(reflect_ref[...], sort, NN, lax.Precision.HIGHEST)
    wide = (rows, GROUP)
    block = (iota(wide, 0) // 4) % 4
    wide_v = jnp.concatenate([sorted_v[:, :32]] * 4 + [sorted_v[:, 32:]] * 4, axis=1)
    wide_v = split3(jnp.where(block == (iota(wide, 1) % LANES) // 32, wide_v, 0.0))
    wide_u = split3(jnp.where(block == iota(wide, 1) // SIZE, jnp.concatenate([u_ref[...]] * 4, axis=1), 0.0))
    to = iota((GROUP, GROUP), 1)
    order = jnp.where(iota((GROUP, GROUP), 0) == ((to % LANES) // 32) * SIZE + (to % 32) * 2 + to // LANES, 1.0, 0.0).astype(F32)
    for g in range(groups):
        at = slice(g * 16, (g + 1) * 16)
        left = jnp.concatenate([wide_u[n][at] for n in (0, 0, 1, 0, 1, 2)], axis=0)
        right = jnp.concatenate([wide_v[n][at] for n in (0, 1, 0, 2, 1, 0)], axis=0)
        high, low = split(order - matmul(left, right, TN))
        high_ref[g] = high
        low_ref[g] = low


def weight_kernel(length, boundary_ref, tab_ref, prev_ref, keep_ref, ktab_ref, turned_ref, decay_ref, weight_ref):
    groups = tab_ref.shape[0]
    keep = jnp.where(boundary_ref[...] == 1, 0.6, 1.0).astype(F32)
    keep_ref[...] = jnp.broadcast_to(keep, (LANES, keep.shape[1])).T

    chunk = keep_ref[pl.ds(0, CHUNKS, stride=length), :]
    for i in range(1, length):
        chunk = chunk * keep_ref[pl.ds(i, CHUNKS, stride=length), :]
    two = chunk * later(chunk, 1, 1.0)
    four = two * later(two, 2, 1.0)
    before = earlier(chunk, 1, 1.0)
    before = before * earlier(before, 1, 1.0)
    before = before * earlier(before, 2, 1.0)
    before = before * earlier(before, 4, 1.0)
    eight = four * later(four, 4, 1.0)
    ktab_ref[0] = chunk
    ktab_ref[1] = two
    ktab_ref[2] = four
    ktab_ref[3] = before
    ktab_ref[4] = jnp.broadcast_to(eight[0:1], TILE)

    one, zero = jnp.ones(TILE, F32), jnp.zeros(TILE, F32)
    for first in range(0, groups, 4):
        some = range(first, min(first + 4, groups))
        states = [entries(tab_ref, ktab_ref, g, None, (one, zero)) for g in some]
        units = [power(tab_ref, g, 0) for g in some]

        def store(k, at, state):
            decay_ref[first + k, 0, at, :] = state[0]
            decay_ref[first + k, 1, at, :] = state[1]

        walk(length, len(some), units, states, keep_ref, None, store)
    for g in range(groups):
        columns = slice(g * GROUP, (g + 1) * GROUP)
        turned = prev_ref[:, columns].T
        turned_ref[columns, :] = turned
        high, low = split(jnp.concatenate([decay_ref[g, 0], decay_ref[g, 1]], axis=1))
        weight_ref[g] = fold(matmul(turned, high) + matmul(turned, low))


VMEM = pl.BlockSpec(memory_space=pltpu.VMEM)
SMEM = pl.BlockSpec(memory_space=pltpu.SMEM)
HBM = pl.BlockSpec(memory_space=pltpu.HBM)


def call(kernel, out_shape, args, specs, scratch=(), flops=0):
    shapes = [jax.ShapeDtypeStruct(s, t) for s, t in out_shape]
    moved = sum(a.size * a.dtype.itemsize for a in args) + sum(s.size * s.dtype.itemsize for s in shapes)
    return pl.pallas_call(
        kernel,
        out_shape=shapes,
        in_specs=specs,
        out_specs=[VMEM] * len(shapes),
        scratch_shapes=list(scratch),
        compiler_params=pltpu.CompilerParams(vmem_limit_bytes=LIMIT),
        cost_estimate=pl.CostEstimate(flops=int(flops), bytes_accessed=int(moved), transcendentals=0),
    )(*args)


def basis(code, reflect, length):
    blocks = reflect.shape[0]
    groups = blocks // 4
    out = [
        ((groups, GROUP, GROUP), BF16),
        ((groups, GROUP, GROUP), BF16),
        ((groups, 2) + TILE, F32),
        ((2, groups, LANES), F32),
    ]
    args = (code, reflect.reshape(blocks * 4, SIZE))
    scratch = [pltpu.VMEM((blocks * 4, SIZE), F32), pltpu.VMEM((blocks, LANES), jnp.int32)]
    return call(functools.partial(basis_kernel, length), out, args, [VMEM] * 2, scratch, groups * 2 * 2 * 256**3)


def weights(boundary, tab, prev):
    groups = tab.shape[0]
    tokens, channels = prev.shape
    out = [
        ((tokens, LANES), F32),
        ((5,) + TILE, F32),
        ((channels, tokens), BF16),
        ((groups, 2, tokens, LANES), F32),
        ((groups, SIZE, GROUP), F32),
    ]
    return call(functools.partial(weight_kernel, tokens // CHUNKS), out, (boundary, tab, prev), [VMEM] * 3, (), groups * 2 * 2 * 256**3)


def scan_kernel(length, base, count, peers, begin, finish, aheads, *refs):
    refs = list(refs)
    take = lambda n: [refs.pop(0) for _ in range(n)]
    tab_ref, ktab_ref, keep_ref = take(3)
    if begin:
        place_ref, own_ref, high_ref, low_ref = take(4)
        others = take(peers - 1)
    if begin and not finish:
        ahead = take(aheads)
    if finish:
        (turned_ref,) = take(1)
    if begin:
        out_ref, head_ref, first_ref = take(3) if not finish else take(1) + [None] + take(1)
    else:
        in_ref, head_ref, out_ref = take(3)
    if finish:
        (grad_ref,) = take(1)
    heads = []
    if begin:
        rows_ref, = take(1)
        spaced_ref = take(1)[0] if finish else out_ref
        size = own_ref.shape[0]
        width = count * GROUP
        place = place_ref[0]
        channels = high_ref.shape[0] * GROUP
        at = pl.ds(pl.multiple_of(place * size, size), size)
        rows_ref[at, :] = own_ref[:, pl.ds(pl.multiple_of(place * channels + base * GROUP, GROUP), width)]
        for k in range(1, peers):
            rows_ref[pl.ds(pl.multiple_of((place ^ k) * size, size), size), :] = others[k - 1][...]
        for n in range(count):
            rows = rows_ref[:, n * GROUP : (n + 1) * GROUP]
            out = matmul(rows, high_ref[base + n]) + matmul(rows, low_ref[base + n])
            spaced_ref[n, 0] = out[:, :LANES]
            spaced_ref[n, 1] = out[:, LANES:]
    else:
        spaced_ref = in_ref
    load = lambda n, at: (spaced_ref[n, 0, at, :], spaced_ref[n, 1, at, :])
    units = [power(tab_ref, base + n, 0) for n in range(count)]
    zero = jnp.zeros(TILE, F32)
    if begin and not finish:
        groups = base + count
        at = 0
        for ref in ahead:
            size = ref.shape[1]
            for c in range(2):
                first_ref[c * groups + at : c * groups + at + size, :] = ref[c]
            at += size
        first_ref[2 * groups :, :] = ktab_ref[4]
    if begin:
        heads = walk(length, count, units, [(zero, zero)] * count, keep_ref, load, None)
        before = ktab_ref[3]
        for n in range(count):
            if head_ref is not None:
                head_ref[n, 0] = heads[n][0]
                head_ref[n, 1] = heads[n][1]
            hop = tuple(jnp.where(iota(TILE, 0) == 0, one, tab_ref[base + n, c]) for c, one in ((0, 1.0), (1, 0.0)))
            moved = times(hop, heads[n])
            for c in range(2):
                value = jnp.sum(moved[c] * before, axis=0, keepdims=True)
                if finish:
                    first_ref[c, n : n + 1, :] = value
                else:
                    first_ref[c * groups + base + n : c * groups + base + n + 1, :] = value
    else:
        heads = [(head_ref[n, 0], head_ref[n, 1]) for n in range(count)]
    if finish:
        states = [entries(tab_ref, ktab_ref, base + n, heads[n], (zero, zero)) for n in range(count)]

        def store(n, at, state):
            out_ref[n, 0, at, :] = state[0]
            out_ref[n, 1, at, :] = state[1]

        walk(length, count, units, states, keep_ref, load, store)
        for n in range(count):
            high, low = split(jnp.concatenate([out_ref[n, 0], out_ref[n, 1]], axis=1))
            turned = turned_ref[(base + n) * GROUP : (base + n + 1) * GROUP, :]
            grad_ref[n] = fold(matmul(turned, high) + matmul(turned, low))


def scan_both(base, count, place, rows, parts, high, low, tab, ktab, keep, turned):
    tokens = keep.shape[0]
    peers = len(parts) + 1
    out = [((count, 2, tokens, LANES), F32), ((2, count, LANES), F32), ((count, SIZE, GROUP), F32)]
    return call(functools.partial(scan_kernel, tokens // CHUNKS, base, count, peers, True, True, 0), out,
                (tab, ktab, keep, place, rows, high, low, *parts, turned), [VMEM] * 3 + [SMEM] + [VMEM] * (peers + 3),
                [pltpu.VMEM((tokens, count * GROUP), BF16), pltpu.VMEM((count, 2, tokens, LANES), F32)], count * 4 * 2 * 256**3)


def scan_first(base, count, place, rows, parts, high, low, tab, ktab, keep, ahead):
    tokens = keep.shape[0]
    peers = len(parts) + 1
    out = [((count, 2, tokens, LANES), F32), ((count, 2) + TILE, F32), ((2 * (base + count) + CHUNKS, LANES), F32)]
    return call(functools.partial(scan_kernel, tokens // CHUNKS, base, count, peers, True, False, len(ahead)), out,
                (tab, ktab, keep, place, rows, high, low, *parts, *ahead), [VMEM] * 3 + [SMEM] + [VMEM] * (peers + 2 + len(ahead)),
                [pltpu.VMEM((tokens, count * GROUP), BF16)], count * 2 * 2 * 256**3)


def scan_second(base, count, spaced, head, tab, ktab, keep, turned):
    tokens = keep.shape[0]
    out = [((count, 2, tokens, LANES), F32), ((count, SIZE, GROUP), F32)]
    return call(functools.partial(scan_kernel, tokens // CHUNKS, base, count, 0, False, True, 0), out,
                (tab, ktab, keep, turned, spaced, head), [VMEM] * 6, (), count * 2 * 2 * 256**3)


def state_kernel(base, sizes, entry_ref, decay_ref, high_ref, low_ref, *refs):
    parts, out_ref = refs[: len(sizes)], refs[-1]
    g = pl.program_id(0) + base
    re, im = entry_ref[0, pl.ds(g, 1), :], entry_ref[1, pl.ds(g, 1), :]
    d_re, d_im = decay_ref[0, 0], decay_ref[0, 1]
    z_re, z_im = parts[0][0, 0], parts[0][0, 1]
    start = 0
    for size, part in zip(sizes[:-1], parts[1:]):
        start += size
        z_re, z_im = jnp.where(g < start, z_re, part[0, 0]), jnp.where(g < start, z_im, part[0, 1])
    z_re = z_re + (re * d_re - im * d_im)
    z_im = z_im + (re * d_im + im * d_re)
    z_high, z_low = split(jnp.concatenate([z_re, z_im], axis=1))
    out = matmul(z_high, high_ref[0], NT) + matmul(z_high, low_ref[0], NT) + matmul(z_low, high_ref[0], NT)
    out_ref[...] = out.astype(BF16)


def states(base, count, parts, decay, entry, high, low, filled=None):
    groups = high.shape[0]
    tokens = parts[0].shape[2]
    sizes = [part.shape[0] for part in parts]
    each = lambda shape: pl.BlockSpec((1,) + shape, lambda g: (g + base, 0, 0, 0)[: len(shape) + 1])

    def pick(start, size):
        return pl.BlockSpec((1, 2, tokens, LANES), lambda g: (jnp.minimum(jnp.maximum(g + base - start, 0), size - 1), 0, 0, 0))

    args = [entry, decay, high, low, *parts]
    specs = [pl.BlockSpec(entry.shape, lambda g: (0, 0, 0)), each((2, tokens, LANES)), each((GROUP, GROUP)), each((GROUP, GROUP))]
    specs += [pick(sum(sizes[:n]), size) for n, size in enumerate(sizes)]
    alias = {}
    if filled is not None:
        alias = {len(args): 0}
        args.append(filled)
        specs.append(pl.BlockSpec(memory_space=pl.ANY))
    return pl.pallas_call(
        functools.partial(state_kernel, base, sizes),
        grid=(count,),
        in_specs=specs,
        out_specs=pl.BlockSpec((tokens, GROUP), lambda g: (0, g + base)),
        out_shape=jax.ShapeDtypeStruct((tokens, groups * GROUP), BF16),
        input_output_aliases=alias,
        name="states",
        compiler_params=pltpu.CompilerParams(vmem_limit_bytes=LIMIT),
        cost_estimate=pl.CostEstimate(flops=count * 3 * 2 * 256**3, bytes_accessed=count * 900_000, transcendentals=0),
    )(*args)


EXTRA = 16
STEPS = 32000.0


def encode(x, code_ref):
    rows = x.shape[0]
    most = jnp.maximum(jnp.max(jnp.abs(x), axis=0, keepdims=True), 1e-30)
    power = jnp.ceil(jnp.log2(most))
    code = jnp.floor(x * (jnp.exp2(-power) * STEPS) + 0.5)
    code_ref[:rows, :] = code.astype(jnp.int32).astype(jnp.int16)
    code_ref[rows:, :] = jnp.broadcast_to(power, (EXTRA, power.shape[1])).astype(jnp.int32).astype(jnp.int16)


def decode(code_ref, start=0, rows=None):
    if rows is None:
        rows = code_ref.shape[0] - EXTRA
    power = code_ref[start + rows : start + rows + EXTRA, :].astype(jnp.int32).astype(F32)[:1]
    return code_ref[start : start + rows, :].astype(jnp.int32).astype(F32) * (jnp.exp2(power) * (1.0 / STEPS))


def merge_kernel(half, side_ref, bit_ref, entry_ref, weight_ref, *refs):
    parts, outs, (own_ref, away_ref) = refs[:-6], refs[-6:-2], refs[-2:]
    blocks = [part.at[n] for part in parts for n in range(part.shape[0])]
    side, bit = side_ref[0], bit_ref[0]
    for n in range(half):
        for out_ref, which in ((own_ref, side), (away_ref, 1 - side)):
            here = jnp.where(which == 0, blocks[n][...], blocks[half + n][...])
            at = which * half + n
            re, im = entry_ref[0, pl.ds(at, 1), :], entry_ref[1, pl.ds(at, 1), :]
            weight = weight_ref[at]
            w_re, w_im = weight[:, :LANES], weight[:, LANES:]
            out_ref[n * SIZE : (n + 1) * SIZE, :LANES] = here[:, :LANES] + (re * w_re - im * w_im)
            out_ref[n * SIZE : (n + 1) * SIZE, LANES:] = here[:, LANES:] + (re * w_im + im * w_re)
    rows = half * SIZE // 2
    here, there = (pl.ds(pl.multiple_of(n * rows, rows), rows) for n in (bit, 1 - bit))
    outs[0][...] = own_ref[here, :]
    outs[1][...] = own_ref[there, :]
    encode(away_ref[here, :], outs[2])
    encode(away_ref[there, :], outs[3])


def merge(half, side, bit, entry, weight, parts):
    rows = half * SIZE // 2
    out = [((rows, GROUP), F32)] * 2 + [((rows + EXTRA, GROUP), jnp.dtype(jnp.int16))] * 2
    return call(functools.partial(merge_kernel, half), out, (side, bit, entry, weight, *parts),
                [SMEM] * 2 + [VMEM] * (2 + len(parts)), [pltpu.VMEM((half * SIZE, GROUP), F32)] * 2)


def add_kernel(*refs):
    total = None
    for ref in refs[:-1]:
        term = ref[...] if ref.dtype == F32 else decode(ref)
        total = term if total is None else total + term
    encode(total, refs[-1])


def add(*terms):
    return call(add_kernel, [(terms[-1].shape, terms[-1].dtype)], terms, [VMEM] * len(terms))[0]


def final_kernel(flips, quarters, side_ref, bit_ref, x_ref, high_ref, low_ref, *refs):
    out_hbm, out_ref, sems = refs[-3:]
    half = high_ref.shape[0] // 2
    count = half * quarters // 2
    side, bit = (1 - ref[0] if flip else ref[0] for ref, flip in zip((side_ref, bit_ref), flips))
    start = side * half + bit * count if quarters == 1 else side * half
    rows = x_ref.shape[0] // quarters - EXTRA
    x = jnp.concatenate([decode(x_ref, n * (rows + EXTRA), rows) for n in range(quarters)], axis=0)
    copies = []
    for n in range(count):
        at = start + n
        x_high, x_low = split(x[n * SIZE : (n + 1) * SIZE, :])
        out = matmul(high_ref[at], x_high, NT) + matmul(low_ref[at], x_high, NT) + matmul(high_ref[at], x_low, NT)
        for j in range(4):
            out_ref[4 * n + j] = out[j * SIZE : (j + 1) * SIZE]
        copies.append(pltpu.make_async_copy(out_ref.at[pl.ds(4 * n, 4)], out_hbm.at[pl.ds(at * 4, 4)], sems.at[n]))
        copies[-1].start()
    for copy in copies:
        copy.wait()


def final(flips, quarters, side, bit, x, high, low, filled=None):
    count = high.shape[0] // 2 * quarters // 2
    blocks = high.shape[0] * 4
    args = [side, bit, x, high, low]
    specs = [SMEM] * 2 + [VMEM] * 3
    alias = {}
    if filled is not None:
        alias = {len(args): 0}
        args.append(filled)
        specs.append(HBM)
    return pl.pallas_call(
        functools.partial(final_kernel, flips, quarters),
        out_shape=jax.ShapeDtypeStruct((blocks, SIZE, SIZE), F32),
        in_specs=specs,
        out_specs=HBM,
        scratch_shapes=[pltpu.VMEM((4 * count, SIZE, SIZE), F32), pltpu.SemaphoreType.DMA((count,))],
        input_output_aliases=alias,
        name="final",
        compiler_params=pltpu.CompilerParams(vmem_limit_bytes=LIMIT),
        cost_estimate=pl.CostEstimate(flops=count * 3 * 2 * 256 * 256 * 64, bytes_accessed=count * 400_000, transcendentals=0),
    )(*args)


def swap(x, axis, k):
    n = lax.axis_size(axis)
    return lax.ppermute(x, axis, [(i, i ^ k) for i in range(n)])


def entering(sent, far, axis, early_bits):
    peers = lax.axis_size(axis)
    rows = far[0].shape[0]
    first, total = (sent[:rows], sent[rows : 2 * rows]), sent[2 * rows : 2 * rows + 1]
    entry = (jnp.zeros_like(first[0]), jnp.zeros_like(first[1]))
    gap = (jnp.ones_like(first[0]), jnp.zeros_like(first[0]))
    k = 1
    for early in early_bits:
        if k > 1:
            sent = jnp.concatenate([first[0], first[1], jnp.broadcast_to(total, (8, LANES))])
        got = swap(sent, axis, k)
        other = (got[:rows], got[rows : 2 * rows])
        other_total = got[2 * rows : 2 * rows + 1]
        reach = times(gap, other)
        entry = tuple(jnp.where(early, e + r, e) for e, r in zip(entry, reach))
        if 2 * k < peers:
            step = times(gap, far)
            gap = tuple(jnp.where(early, other_total * s, g) for s, g in zip(step, gap))
            near = tuple(jnp.where(early, a, b) for a, b in zip(first, other))
            late = tuple(jnp.where(early, b, a) for a, b in zip(first, other))
            moved = times(far, late)
            first = tuple(a + jnp.where(early, total, other_total) * b for a, b in zip(near, moved))
            total = total * other_total
            far = times(far, far)
        k *= 2
    return jnp.stack(entry)


def exchanges(axes):
    steps = []
    for axis in axes:
        k = 1
        while k < lax.axis_size(axis):
            steps.append((axis, k))
            k *= 2
    return steps


def bits(steps):
    return [(lax.axis_index(axis).astype(jnp.uint32) // jnp.uint32(k)) & jnp.uint32(1) for axis, k in steps]


def total_sum(quarters, steps):
    own_here, own_there, away_here, away_there = quarters
    got = swap(away_there, *steps[0])
    code = add(own_there, got)
    near = swap(away_here, *steps[0])
    got = swap(code, *steps[1])
    code = add(own_here, near, got)
    for step in steps[2:]:
        got = swap(code, *step)
        code = add(code, got)
    return code


def spread(code, steps, side, bit, lower, high, low):
    other = swap(code, *steps[1])
    if high.shape[0] % 4:
        both = jnp.where(lower, jnp.concatenate([code, other]), jnp.concatenate([other, code]))
        away = swap(both, *steps[0])
        out = final((False, False), 2, side, bit, both, high, low)
        return final((True, False), 2, side, bit, away, high, low, out)
    near = swap(code, *steps[0])
    out = final((False, False), 1, side, bit, code, high, low)
    out = final((True, False), 1, side, bit, near, high, low, out)
    far = swap(other, *steps[0])
    out = final((False, True), 1, side, bit, other, high, low, out)
    return final((True, True), 1, side, bit, far, high, low, out)


def inner(out_grad, prev_state, boundary, angle_code, radius_code, reflect):
    peers, place = lax.axis_size("tensor"), lax.axis_index("tensor")
    rows = out_grad[0]
    channels = prev_state.shape[2]
    tokens = prev_state.shape[1]
    groups = channels // GROUP
    half = groups // 2
    counts = [max(1, groups * 5 // 8)]
    counts.append(groups - counts[0])
    bases = [sum(counts[:n]) for n in range(len(counts))]
    place = place.astype(jnp.uint32)

    def away(k, base, count):
        start = (place ^ jnp.uint32(k)) * jnp.uint32(channels) + jnp.uint32(base * GROUP)
        return lax.dynamic_slice(rows, (jnp.uint32(0), start), (rows.shape[0], count * GROUP))

    parts = []
    for at in zip(bases, counts):
        parts.append([swap(away(k, *at), "tensor", k) for k in range(1, peers)])
    steps = exchanges(("dp", "ctx"))
    bit = bits(steps)[1]
    lower = bit == 0
    bit = jnp.reshape(bit.astype(jnp.int32), (1,))
    side = jnp.reshape(lax.axis_index("dp") & 1, (1,))
    place = jnp.reshape(place.astype(jnp.int32), (1,))
    early = [bit == 0 for bit in bits(exchanges(("ctx",)))]
    code = angle_code * 1024 + radius_code
    code, side, place, bit, lower, early = lax.optimization_barrier((code, side, place, bit, lower, early))
    high, low, tab, far = basis(code, reflect, tokens // CHUNKS)
    keep, ktab, turned, decay, weight = weights(boundary, tab, prev_state[0])
    done = []
    for base, count, part in zip(bases[:-1], counts[:-1], parts[:-1]):
        done.append(scan_both(base, count, place, rows, part, high, low, tab, ktab, keep, turned))
    base, count = bases[-1], counts[-1]
    spaced, head, sent = scan_first(base, count, place, rows, parts[-1], high, low, tab, ktab, keep, [d[1] for d in done])
    entry = entering(sent, (far[0], far[1]), "ctx", early)
    z_last, grad_last = scan_second(base, count, spaced, head, tab, ktab, keep, turned)
    quarters = merge(half, side, bit, entry, weight, [d[2] for d in done] + [grad_last])
    z = [d[0] for d in done] + [z_last]
    grad_input = None
    for base, count in shares(groups):
        if count:
            grad_input = states(base, count, z, decay, entry, high, low, grad_input)
    grad_transition = spread(total_sum(quarters, steps), steps, side, bit, lower, high, low)
    return grad_input[None], grad_transition


def shares(groups):
    counts = [groups // 4]
    counts.append((groups - counts[0] + 1) // 2)
    counts.append(groups - sum(counts))
    return [(sum(counts[:n]), count) for n, count in enumerate(counts)]


def solution(mesh):
    in_specs = (
        P("dp", ("ctx", "tensor"), None),
        P("dp", "ctx", "tensor"),
        P("dp", "ctx"),
        P("tensor", None),
        P("tensor", None),
        P("tensor", None, None),
    )
    out_specs = (P("dp", "ctx", "tensor"), P("tensor", None, None))
    return jax.shard_map(inner, mesh=mesh, in_specs=in_specs, out_specs=out_specs, check_vma=False)
```

```python
import functools
import math

import jax
import jax.numpy as jnp
from jax import lax
from jax.experimental import pallas as pl
from jax.experimental.pallas import tpu as pltpu
from jax.sharding import PartitionSpec as P


F32 = jnp.float32
BF16 = jnp.bfloat16
LANES = 128
CHUNKS = 8
GROUP = 256
SIZE = 64
TILE = (CHUNKS, LANES)
LIMIT = 16 << 20
NN = ((1,), (0,))
NT = ((1,), (1,))
TN = ((0,), (0,))


def iota(shape, dim):
    return lax.broadcasted_iota(jnp.int32, shape, dim)


def matmul(a, b, dims=NN, precision=None):
    return lax.dot_general(a, b, (dims, ((), ())), precision=precision, preferred_element_type=F32)


def split(x):
    high = x.astype(BF16)
    return high, (x - high.astype(F32)).astype(BF16)


def split3(x):
    high = x.astype(BF16)
    rest = x - high.astype(F32)
    middle = rest.astype(BF16)
    return high, middle, (rest - middle.astype(F32)).astype(BF16)


def times(a, b):
    return a[0] * b[0] - a[1] * b[1], a[0] * b[1] + a[1] * b[0]


def later(x, k, fill):
    return jnp.where(iota(TILE, 0) < CHUNKS - k, pltpu.roll(x, CHUNKS - k, 0), fill)


def earlier(x, k, fill):
    return jnp.where(iota(TILE, 0) >= k, pltpu.roll(x, k, 0), fill)


def power(tab_ref, g, n):
    return tuple(jnp.broadcast_to(tab_ref[g, c, n : n + 1], TILE) for c in range(2))


def entries(tab_ref, ktab_ref, g, head, entry):
    last = iota(TILE, 0) == CHUNKS - 1
    moved = times(power(tab_ref, g, 1), entry)
    scan = tuple(jnp.where(last, ktab_ref[0] * m, 0.0) for m in moved)
    if head is not None:
        scan = tuple(h + s for h, s in zip(head, scan))
    for n in range(3):
        near = tuple(later(x, 1 << n, 0.0) for x in scan)
        moved = times(power(tab_ref, g, 1 << n), near)
        scan = tuple(s + ktab_ref[n] * m for s, m in zip(scan, moved))
    return tuple(jnp.where(last, e, pltpu.roll(s, CHUNKS - 1, 0)) for e, s in zip(entry, scan))


def fold(x):
    block = (iota((SIZE, GROUP), 1) % LANES) // 32
    out = x[:SIZE]
    for j in range(1, 4):
        out = jnp.where(block == j, x[j * SIZE : (j + 1) * SIZE], out)
    return out


def walk(length, groups, units, states, keep_ref, load, store):
    for i in range(length - 1, -1, -1):
        at = pl.ds(i, CHUNKS, stride=length)
        keep = keep_ref[at, :]
        for n in range(groups):
            re, im = states[n]
            step_re, step_im = keep * units[n][0], keep * units[n][1]
            if load is None:
                states[n] = (step_re * re - step_im * im, step_re * im + step_im * re)
            else:
                a, b = load(n, at)
                states[n] = ((a + step_re * re) - step_im * im, (b + step_re * im) + step_im * re)
            if store is not None:
                store(n, at, states[n])
    return states


def basis_kernel(length, code_ref, reflect_ref, high_ref, low_ref, tab_ref, far_ref, u_ref, wide_ref):
    rows = reflect_ref.shape[0]
    blocks = rows // 4
    groups = blocks // 4

    wide_ref[...] = jnp.concatenate([code_ref[...]] * 4, axis=1)
    codes = wide_ref[pl.ds(0, groups, stride=4), :]
    block = iota(codes.shape, 1) // 32
    for j in range(1, 4):
        codes = jnp.where(block == j, wide_ref[pl.ds(j, groups, stride=4), :], codes)

    rates = jnp.exp(-math.log(2.0) * (4.0 + (codes & 1023).astype(F32) * (10.0 / 1024.0)))
    series = jnp.full_like(rates, 1.0 / 8.0)
    for k in range(7, 0, -1):
        series = series * rates + 1.0 / k
    logs = -rates * series
    angles = codes >> 10
    row = iota(TILE, 0)
    n = jnp.where(row == 0, 1, row * length)
    for g in range(groups):
        turn = ((n * angles[g : g + 1, :]) & 8191).astype(F32) * (math.pi / 4096.0)
        size = jnp.exp(n.astype(F32) * logs[g : g + 1, :])
        re, im = size * jnp.cos(turn), -size * jnp.sin(turn)
        tab_ref[g, 0] = re
        tab_ref[g, 1] = im
        half = (re[4:5], im[4:5])
        whole = times(half, half)
        far_ref[0, g : g + 1, :] = whole[0]
        far_ref[1, g : g + 1, :] = whole[1]

    v = [reflect_ref[pl.ds(k, blocks, stride=4), :] for k in range(4)]
    u = []
    for k in range(4):
        now = v[k]
        for l in range(k):
            now = now - u[l] * jnp.sum(v[l] * v[k], axis=1, keepdims=True)
        u.append(now * (2.0 / jnp.sum(v[k] * v[k], axis=1, keepdims=True)))
        u_ref[pl.ds(k, blocks, stride=4), :] = u[k]
    to = iota((SIZE, SIZE), 1)
    sort = jnp.where(iota((SIZE, SIZE), 0) == (to % 32) * 2 + to // 32, 1.0, 0.0).astype(F32)
    sorted_v = matmul(reflect_ref[...], sort, NN, lax.Precision.HIGHEST)
    wide = (rows, GROUP)
    block = (iota(wide, 0) // 4) % 4
    wide_v = jnp.concatenate([sorted_v[:, :32]] * 4 + [sorted_v[:, 32:]] * 4, axis=1)
    wide_v = split3(jnp.where(block == (iota(wide, 1) % LANES) // 32, wide_v, 0.0))
    wide_u = split3(jnp.where(block == iota(wide, 1) // SIZE, jnp.concatenate([u_ref[...]] * 4, axis=1), 0.0))
    to = iota((GROUP, GROUP), 1)
    order = jnp.where(iota((GROUP, GROUP), 0) == ((to % LANES) // 32) * SIZE + (to % 32) * 2 + to // LANES, 1.0, 0.0).astype(F32)
    for g in range(groups):
        at = slice(g * 16, (g + 1) * 16)
        left = jnp.concatenate([wide_u[n][at] for n in (0, 0, 1, 0, 1, 2)], axis=0)
        right = jnp.concatenate([wide_v[n][at] for n in (0, 1, 0, 2, 1, 0)], axis=0)
        high, low = split(order - matmul(left, right, TN))
        high_ref[g] = high
        low_ref[g] = low


def weight_kernel(length, boundary_ref, tab_ref, prev_ref, keep_ref, ktab_ref, turned_ref, decay_ref, weight_ref):
    groups = tab_ref.shape[0]
    keep = jnp.where(boundary_ref[...] == 1, 0.6, 1.0).astype(F32)
    keep_ref[...] = jnp.broadcast_to(keep, (LANES, keep.shape[1])).T

    chunk = keep_ref[pl.ds(0, CHUNKS, stride=length), :]
    for i in range(1, length):
        chunk = chunk * keep_ref[pl.ds(i, CHUNKS, stride=length), :]
    two = chunk * later(chunk, 1, 1.0)
    four = two * later(two, 2, 1.0)
    before = earlier(chunk, 1, 1.0)
    before = before * earlier(before, 1, 1.0)
    before = before * earlier(before, 2, 1.0)
    before = before * earlier(before, 4, 1.0)
    eight = four * later(four, 4, 1.0)
    ktab_ref[0] = chunk
    ktab_ref[1] = two
    ktab_ref[2] = four
    ktab_ref[3] = before
    ktab_ref[4] = jnp.broadcast_to(eight[0:1], TILE)

    one, zero = jnp.ones(TILE, F32), jnp.zeros(TILE, F32)
    for first in range(0, groups, 4):
        some = range(first, min(first + 4, groups))
        states = [entries(tab_ref, ktab_ref, g, None, (one, zero)) for g in some]
        units = [power(tab_ref, g, 0) for g in some]

        def store(k, at, state):
            decay_ref[first + k, 0, at, :] = state[0]
            decay_ref[first + k, 1, at, :] = state[1]

        walk(length, len(some), units, states, keep_ref, None, store)
    for g in range(groups):
        columns = slice(g * GROUP, (g + 1) * GROUP)
        turned = prev_ref[:, columns].T
        turned_ref[columns, :] = turned
        high, low = split(jnp.concatenate([decay_ref[g, 0], decay_ref[g, 1]], axis=1))
        weight_ref[g] = fold(matmul(turned, high) + matmul(turned, low))


VMEM = pl.BlockSpec(memory_space=pltpu.VMEM)
SMEM = pl.BlockSpec(memory_space=pltpu.SMEM)
HBM = pl.BlockSpec(memory_space=pltpu.HBM)


def call(kernel, out_shape, args, specs, scratch=(), flops=0):
    shapes = [jax.ShapeDtypeStruct(s, t) for s, t in out_shape]
    moved = sum(a.size * a.dtype.itemsize for a in args) + sum(s.size * s.dtype.itemsize for s in shapes)
    return pl.pallas_call(
        kernel,
        out_shape=shapes,
        in_specs=specs,
        out_specs=[VMEM] * len(shapes),
        scratch_shapes=list(scratch),
        compiler_params=pltpu.CompilerParams(vmem_limit_bytes=LIMIT),
        cost_estimate=pl.CostEstimate(flops=int(flops), bytes_accessed=int(moved), transcendentals=0),
    )(*args)


def basis(code, reflect, length):
    blocks = reflect.shape[0]
    groups = blocks // 4
    out = [
        ((groups, GROUP, GROUP), BF16),
        ((groups, GROUP, GROUP), BF16),
        ((groups, 2) + TILE, F32),
        ((2, groups, LANES), F32),
    ]
    args = (code, reflect.reshape(blocks * 4, SIZE))
    scratch = [pltpu.VMEM((blocks * 4, SIZE), F32), pltpu.VMEM((blocks, LANES), jnp.int32)]
    return call(functools.partial(basis_kernel, length), out, args, [VMEM] * 2, scratch, groups * 2 * 2 * 256**3)


def weights(boundary, tab, prev):
    groups = tab.shape[0]
    tokens, channels = prev.shape
    out = [
        ((tokens, LANES), F32),
        ((5,) + TILE, F32),
        ((channels, tokens), BF16),
        ((groups, 2, tokens, LANES), F32),
        ((groups, SIZE, GROUP), F32),
    ]
    return call(functools.partial(weight_kernel, tokens // CHUNKS), out, (boundary, tab, prev), [VMEM] * 3, (), groups * 2 * 2 * 256**3)


def scan_kernel(length, base, count, peers, begin, finish, aheads, *refs):
    refs = list(refs)
    take = lambda n: [refs.pop(0) for _ in range(n)]
    tab_ref, ktab_ref, keep_ref = take(3)
    if begin:
        place_ref, own_ref, high_ref, low_ref = take(4)
        others = take(peers - 1)
    if begin and not finish:
        ahead = take(aheads)
    if finish:
        (turned_ref,) = take(1)
    if begin:
        out_ref, head_ref, first_ref = take(3) if not finish else take(1) + [None] + take(1)
    else:
        in_ref, head_ref, out_ref = take(3)
    if finish:
        (grad_ref,) = take(1)
    heads = []
    if begin:
        rows_ref, = take(1)
        spaced_ref = take(1)[0] if finish else out_ref
        size = own_ref.shape[0]
        width = count * GROUP
        place = place_ref[0]
        channels = high_ref.shape[0] * GROUP
        at = pl.ds(pl.multiple_of(place * size, size), size)
        rows_ref[at, :] = own_ref[:, pl.ds(pl.multiple_of(place * channels + base * GROUP, GROUP), width)]
        for k in range(1, peers):
            rows_ref[pl.ds(pl.multiple_of((place ^ k) * size, size), size), :] = others[k - 1][...]
        for n in range(count):
            rows = rows_ref[:, n * GROUP : (n + 1) * GROUP]
            out = matmul(rows, high_ref[base + n]) + matmul(rows, low_ref[base + n])
            spaced_ref[n, 0] = out[:, :LANES]
            spaced_ref[n, 1] = out[:, LANES:]
    else:
        spaced_ref = in_ref
    load = lambda n, at: (spaced_ref[n, 0, at, :], spaced_ref[n, 1, at, :])
    units = [power(tab_ref, base + n, 0) for n in range(count)]
    zero = jnp.zeros(TILE, F32)
    if begin and not finish:
        groups = base + count
        at = 0
        for ref in ahead:
            size = ref.shape[1]
            for c in range(2):
                first_ref[c * groups + at : c * groups + at + size, :] = ref[c]
            at += size
        first_ref[2 * groups :, :] = ktab_ref[4]
    if begin:
        heads = walk(length, count, units, [(zero, zero)] * count, keep_ref, load, None)
        before = ktab_ref[3]
        for n in range(count):
            if head_ref is not None:
                head_ref[n, 0] = heads[n][0]
                head_ref[n, 1] = heads[n][1]
            hop = tuple(jnp.where(iota(TILE, 0) == 0, one, tab_ref[base + n, c]) for c, one in ((0, 1.0), (1, 0.0)))
            moved = times(hop, heads[n])
            for c in range(2):
                value = jnp.sum(moved[c] * before, axis=0, keepdims=True)
                if finish:
                    first_ref[c, n : n + 1, :] = value
                else:
                    first_ref[c * groups + base + n : c * groups + base + n + 1, :] = value
    else:
        heads = [(head_ref[n, 0], head_ref[n, 1]) for n in range(count)]
    if finish:
        states = [entries(tab_ref, ktab_ref, base + n, heads[n], (zero, zero)) for n in range(count)]

        def store(n, at, state):
            out_ref[n, 0, at, :] = state[0]
            out_ref[n, 1, at, :] = state[1]

        walk(length, count, units, states, keep_ref, load, store)
        for n in range(count):
            high, low = split(jnp.concatenate([out_ref[n, 0], out_ref[n, 1]], axis=1))
            turned = turned_ref[(base + n) * GROUP : (base + n + 1) * GROUP, :]
            grad_ref[n] = fold(matmul(turned, high) + matmul(turned, low))


def scan_both(base, count, place, rows, parts, high, low, tab, ktab, keep, turned):
    tokens = keep.shape[0]
    peers = len(parts) + 1
    out = [((count, 2, tokens, LANES), F32), ((2, count, LANES), F32), ((count, SIZE, GROUP), F32)]
    return call(functools.partial(scan_kernel, tokens // CHUNKS, base, count, peers, True, True, 0), out,
                (tab, ktab, keep, place, rows, high, low, *parts, turned), [VMEM] * 3 + [SMEM] + [VMEM] * (peers + 3),
                [pltpu.VMEM((tokens, count * GROUP), BF16), pltpu.VMEM((count, 2, tokens, LANES), F32)], count * 4 * 2 * 256**3)


def scan_first(base, count, place, rows, parts, high, low, tab, ktab, keep, ahead):
    tokens = keep.shape[0]
    peers = len(parts) + 1
    out = [((count, 2, tokens, LANES), F32), ((count, 2) + TILE, F32), ((2 * (base + count) + CHUNKS, LANES), F32)]
    return call(functools.partial(scan_kernel, tokens // CHUNKS, base, count, peers, True, False, len(ahead)), out,
                (tab, ktab, keep, place, rows, high, low, *parts, *ahead), [VMEM] * 3 + [SMEM] + [VMEM] * (peers + 2 + len(ahead)),
                [pltpu.VMEM((tokens, count * GROUP), BF16)], count * 2 * 2 * 256**3)


def scan_second(base, count, spaced, head, tab, ktab, keep, turned):
    tokens = keep.shape[0]
    out = [((count, 2, tokens, LANES), F32), ((count, SIZE, GROUP), F32)]
    return call(functools.partial(scan_kernel, tokens // CHUNKS, base, count, 0, False, True, 0), out,
                (tab, ktab, keep, turned, spaced, head), [VMEM] * 6, (), count * 2 * 2 * 256**3)


def state_kernel(base, sizes, entry_ref, decay_ref, high_ref, low_ref, *refs):
    parts, out_ref = refs[: len(sizes)], refs[-1]
    g = pl.program_id(0) + base
    re, im = entry_ref[0, pl.ds(g, 1), :], entry_ref[1, pl.ds(g, 1), :]
    d_re, d_im = decay_ref[0, 0], decay_ref[0, 1]
    z_re, z_im = parts[0][0, 0], parts[0][0, 1]
    start = 0
    for size, part in zip(sizes[:-1], parts[1:]):
        start += size
        z_re, z_im = jnp.where(g < start, z_re, part[0, 0]), jnp.where(g < start, z_im, part[0, 1])
    z_re = z_re + (re * d_re - im * d_im)
    z_im = z_im + (re * d_im + im * d_re)
    z_high, z_low = split(jnp.concatenate([z_re, z_im], axis=1))
    out = matmul(z_high, high_ref[0], NT) + matmul(z_high, low_ref[0], NT) + matmul(z_low, high_ref[0], NT)
    out_ref[...] = out.astype(BF16)


def states(base, count, parts, decay, entry, high, low, filled=None):
    groups = high.shape[0]
    tokens = parts[0].shape[2]
    sizes = [part.shape[0] for part in parts]
    each = lambda shape: pl.BlockSpec((1,) + shape, lambda g: (g + base, 0, 0, 0)[: len(shape) + 1])

    def pick(start, size):
        return pl.BlockSpec((1, 2, tokens, LANES), lambda g: (jnp.minimum(jnp.maximum(g + base - start, 0), size - 1), 0, 0, 0))

    args = [entry, decay, high, low, *parts]
    specs = [pl.BlockSpec(entry.shape, lambda g: (0, 0, 0)), each((2, tokens, LANES)), each((GROUP, GROUP)), each((GROUP, GROUP))]
    specs += [pick(sum(sizes[:n]), size) for n, size in enumerate(sizes)]
    alias = {}
    if filled is not None:
        alias = {len(args): 0}
        args.append(filled)
        specs.append(pl.BlockSpec(memory_space=pl.ANY))
    return pl.pallas_call(
        functools.partial(state_kernel, base, sizes),
        grid=(count,),
        in_specs=specs,
        out_specs=pl.BlockSpec((tokens, GROUP), lambda g: (0, g + base)),
        out_shape=jax.ShapeDtypeStruct((tokens, groups * GROUP), BF16),
        input_output_aliases=alias,
        name="states",
        compiler_params=pltpu.CompilerParams(vmem_limit_bytes=LIMIT),
        cost_estimate=pl.CostEstimate(flops=count * 3 * 2 * 256**3, bytes_accessed=count * 900_000, transcendentals=0),
    )(*args)


STEPS = 32000.0
LEAST = -100


def encode(x, code_ref):
    most = jnp.max(jnp.abs(x), axis=0, keepdims=True)
    power = jnp.ceil(jnp.log2(jnp.maximum(most, 2.0**LEAST)))
    code = jnp.floor(x * (jnp.exp2(-power) * STEPS) + 0.5).astype(jnp.int32)
    row = iota((16, x.shape[1]), 0)
    bit = ((power - LEAST).astype(jnp.int32) >> row) & 1
    first = jnp.where(row < 8, (code[:16] & -2) | bit, code[:16])
    code_ref[:16, :] = first.astype(jnp.int16)
    code_ref[16:, :] = code[16:].astype(jnp.int16)


def decode(code_ref, start=0, rows=None):
    rows = code_ref.shape[0] if rows is None else rows
    first = code_ref[start : start + 16, :].astype(jnp.int32)
    row = iota(first.shape, 0)
    bits = jnp.where(row < 8, (first & 1) << row, 0).astype(F32)
    power = jnp.sum(bits, axis=0, keepdims=True) + float(LEAST)
    return code_ref[start : start + rows, :].astype(jnp.int32).astype(F32) * (jnp.exp2(power) * (1.0 / STEPS))


def merge_kernel(half, side_ref, bit_ref, entry_ref, weight_ref, *refs):
    parts, outs, (own_ref, away_ref) = refs[:-6], refs[-6:-2], refs[-2:]
    blocks = [part.at[n] for part in parts for n in range(part.shape[0])]
    side, bit = side_ref[0], bit_ref[0]
    for n in range(half):
        for out_ref, which in ((own_ref, side), (away_ref, 1 - side)):
            here = jnp.where(which == 0, blocks[n][...], blocks[half + n][...])
            at = which * half + n
            re, im = entry_ref[0, pl.ds(at, 1), :], entry_ref[1, pl.ds(at, 1), :]
            weight = weight_ref[at]
            w_re, w_im = weight[:, :LANES], weight[:, LANES:]
            out_ref[n * SIZE : (n + 1) * SIZE, :LANES] = here[:, :LANES] + (re * w_re - im * w_im)
            out_ref[n * SIZE : (n + 1) * SIZE, LANES:] = here[:, LANES:] + (re * w_im + im * w_re)
    rows = half * SIZE // 2
    here, there = (pl.ds(pl.multiple_of(n * rows, rows), rows) for n in (bit, 1 - bit))
    outs[0][...] = own_ref[here, :]
    outs[1][...] = own_ref[there, :]
    encode(away_ref[here, :], outs[2])
    encode(away_ref[there, :], outs[3])


def merge(half, side, bit, entry, weight, parts):
    rows = half * SIZE // 2
    out = [((rows, GROUP), F32)] * 2 + [((rows, GROUP), jnp.dtype(jnp.int16))] * 2
    return call(functools.partial(merge_kernel, half), out, (side, bit, entry, weight, *parts),
                [SMEM] * 2 + [VMEM] * (2 + len(parts)), [pltpu.VMEM((half * SIZE, GROUP), F32)] * 2)


def add_kernel(*refs):
    total = None
    for ref in refs[:-1]:
        term = ref[...] if ref.dtype == F32 else decode(ref)
        total = term if total is None else total + term
    encode(total, refs[-1])


def add(*terms):
    return call(add_kernel, [(terms[-1].shape, terms[-1].dtype)], terms, [VMEM] * len(terms))[0]


def final_kernel(flips, quarters, side_ref, bit_ref, x_ref, high_ref, low_ref, *refs):
    out_hbm, out_ref, sems = refs[-3:]
    half = high_ref.shape[0] // 2
    count = half * quarters // 2
    side, bit = (1 - ref[0] if flip else ref[0] for ref, flip in zip((side_ref, bit_ref), flips))
    start = side * half + bit * count if quarters == 1 else side * half
    rows = x_ref.shape[0] // quarters
    x = jnp.concatenate([decode(x_ref, n * rows, rows) for n in range(quarters)], axis=0)
    copies = []
    for n in range(count):
        at = start + n
        x_high, x_low = split(x[n * SIZE : (n + 1) * SIZE, :])
        out = matmul(high_ref[at], x_high, NT) + matmul(low_ref[at], x_high, NT) + matmul(high_ref[at], x_low, NT)
        for j in range(4):
            out_ref[4 * n + j] = out[j * SIZE : (j + 1) * SIZE]
        copies.append(pltpu.make_async_copy(out_ref.at[pl.ds(4 * n, 4)], out_hbm.at[pl.ds(at * 4, 4)], sems.at[n]))
        copies[-1].start()
    for copy in copies:
        copy.wait()


def final(flips, quarters, side, bit, x, high, low, filled=None):
    count = high.shape[0] // 2 * quarters // 2
    blocks = high.shape[0] * 4
    args = [side, bit, x, high, low]
    specs = [SMEM] * 2 + [VMEM] * 3
    alias = {}
    if filled is not None:
        alias = {len(args): 0}
        args.append(filled)
        specs.append(HBM)
    return pl.pallas_call(
        functools.partial(final_kernel, flips, quarters),
        out_shape=jax.ShapeDtypeStruct((blocks, SIZE, SIZE), F32),
        in_specs=specs,
        out_specs=HBM,
        scratch_shapes=[pltpu.VMEM((4 * count, SIZE, SIZE), F32), pltpu.SemaphoreType.DMA((count,))],
        input_output_aliases=alias,
        name="final",
        compiler_params=pltpu.CompilerParams(vmem_limit_bytes=LIMIT),
        cost_estimate=pl.CostEstimate(flops=count * 3 * 2 * 256 * 256 * 64, bytes_accessed=count * 400_000, transcendentals=0),
    )(*args)


def swap(x, axis, k):
    n = lax.axis_size(axis)
    return lax.ppermute(x, axis, [(i, i ^ k) for i in range(n)])


def entering(sent, far, axis, early_bits):
    peers = lax.axis_size(axis)
    rows = far[0].shape[0]
    first, total = (sent[:rows], sent[rows : 2 * rows]), sent[2 * rows : 2 * rows + 1]
    entry = (jnp.zeros_like(first[0]), jnp.zeros_like(first[1]))
    gap = (jnp.ones_like(first[0]), jnp.zeros_like(first[0]))
    k = 1
    for early in early_bits:
        if k > 1:
            sent = jnp.concatenate([first[0], first[1], jnp.broadcast_to(total, (8, LANES))])
        got = swap(sent, axis, k)
        other = (got[:rows], got[rows : 2 * rows])
        other_total = got[2 * rows : 2 * rows + 1]
        reach = times(gap, other)
        entry = tuple(jnp.where(early, e + r, e) for e, r in zip(entry, reach))
        if 2 * k < peers:
            step = times(gap, far)
            gap = tuple(jnp.where(early, other_total * s, g) for s, g in zip(step, gap))
            near = tuple(jnp.where(early, a, b) for a, b in zip(first, other))
            late = tuple(jnp.where(early, b, a) for a, b in zip(first, other))
            moved = times(far, late)
            first = tuple(a + jnp.where(early, total, other_total) * b for a, b in zip(near, moved))
            total = total * other_total
            far = times(far, far)
        k *= 2
    return jnp.stack(entry)


def exchanges(axes):
    steps = []
    for axis in axes:
        k = 1
        while k < lax.axis_size(axis):
            steps.append((axis, k))
            k *= 2
    return steps


def bits(steps):
    return [(lax.axis_index(axis).astype(jnp.uint32) // jnp.uint32(k)) & jnp.uint32(1) for axis, k in steps]


def total_sum(quarters, steps):
    own_here, own_there, away_here, away_there = quarters
    got = swap(away_there, *steps[0])
    code = add(own_there, got)
    near = swap(away_here, *steps[0])
    got = swap(code, *steps[1])
    code = add(own_here, near, got)
    for step in steps[2:]:
        got = swap(code, *step)
        code = add(code, got)
    return code


def spread(code, steps, side, bit, lower, high, low):
    other = swap(code, *steps[1])
    if high.shape[0] % 4:
        both = jnp.where(lower, jnp.concatenate([code, other]), jnp.concatenate([other, code]))
        away = swap(both, *steps[0])
        out = final((False, False), 2, side, bit, both, high, low)
        return final((True, False), 2, side, bit, away, high, low, out)
    near = swap(code, *steps[0])
    out = final((False, False), 1, side, bit, code, high, low)
    out = final((True, False), 1, side, bit, near, high, low, out)
    far = swap(other, *steps[0])
    out = final((False, True), 1, side, bit, other, high, low, out)
    return final((True, True), 1, side, bit, far, high, low, out)


def inner(out_grad, prev_state, boundary, angle_code, radius_code, reflect):
    peers, place = lax.axis_size("tensor"), lax.axis_index("tensor")
    rows = out_grad[0]
    channels = prev_state.shape[2]
    tokens = prev_state.shape[1]
    groups = channels // GROUP
    half = groups // 2
    counts = [max(1, groups * 5 // 8)]
    counts.append(groups - counts[0])
    bases = [sum(counts[:n]) for n in range(len(counts))]
    place = place.astype(jnp.uint32)

    def away(k, base, count):
        start = (place ^ jnp.uint32(k)) * jnp.uint32(channels) + jnp.uint32(base * GROUP)
        return lax.dynamic_slice(rows, (jnp.uint32(0), start), (rows.shape[0], count * GROUP))

    parts = []
    for at in zip(bases, counts):
        parts.append([swap(away(k, *at), "tensor", k) for k in range(1, peers)])
    steps = exchanges(("dp", "ctx"))
    bit = bits(steps)[1]
    lower = bit == 0
    bit = jnp.reshape(bit.astype(jnp.int32), (1,))
    side = jnp.reshape(lax.axis_index("dp") & 1, (1,))
    place = jnp.reshape(place.astype(jnp.int32), (1,))
    early = [bit == 0 for bit in bits(exchanges(("ctx",)))]
    code = angle_code * 1024 + radius_code
    code, side, place, bit, lower, early = lax.optimization_barrier((code, side, place, bit, lower, early))
    high, low, tab, far = basis(code, reflect, tokens // CHUNKS)
    keep, ktab, turned, decay, weight = weights(boundary, tab, prev_state[0])
    done = []
    for base, count, part in zip(bases[:-1], counts[:-1], parts[:-1]):
        done.append(scan_both(base, count, place, rows, part, high, low, tab, ktab, keep, turned))
    base, count = bases[-1], counts[-1]
    spaced, head, sent = scan_first(base, count, place, rows, parts[-1], high, low, tab, ktab, keep, [d[1] for d in done])
    entry = entering(sent, (far[0], far[1]), "ctx", early)
    z_last, grad_last = scan_second(base, count, spaced, head, tab, ktab, keep, turned)
    quarters = merge(half, side, bit, entry, weight, [d[2] for d in done] + [grad_last])
    z = [d[0] for d in done] + [z_last]
    grad_input = None
    for base, count in shares(groups):
        if count:
            grad_input = states(base, count, z, decay, entry, high, low, grad_input)
    grad_transition = spread(total_sum(quarters, steps), steps, side, bit, lower, high, low)
    return grad_input[None], grad_transition


def shares(groups):
    counts = [groups // 4]
    counts.append((groups - counts[0] + 1) // 2)
    counts.append(groups - sum(counts))
    return [(sum(counts[:n]), count) for n, count in enumerate(counts)]


def solution(mesh):
    in_specs = (
        P("dp", ("ctx", "tensor"), None),
        P("dp", "ctx", "tensor"),
        P("dp", "ctx"),
        P("tensor", None),
        P("tensor", None),
        P("tensor", None, None),
    )
    out_specs = (P("dp", "ctx", "tensor"), P("tensor", None, None))
    return jax.shard_map(inner, mesh=mesh, in_specs=in_specs, out_specs=out_specs, check_vma=False)
```

```python
import functools
import math

import jax
import jax.numpy as jnp
from jax import lax
from jax.experimental import pallas as pl
from jax.experimental.pallas import tpu as pltpu
from jax.sharding import PartitionSpec as P


F32 = jnp.float32
BF16 = jnp.bfloat16
LANES = 128
CHUNKS = 8
GROUP = 256
SIZE = 64
TILE = (CHUNKS, LANES)
LIMIT = 16 << 20
NN = ((1,), (0,))
NT = ((1,), (1,))
TN = ((0,), (0,))


def iota(shape, dim):
    return lax.broadcasted_iota(jnp.int32, shape, dim)


def matmul(a, b, dims=NN, precision=None):
    return lax.dot_general(a, b, (dims, ((), ())), precision=precision, preferred_element_type=F32)


def split(x):
    high = x.astype(BF16)
    return high, (x - high.astype(F32)).astype(BF16)


def split3(x):
    high = x.astype(BF16)
    rest = x - high.astype(F32)
    middle = rest.astype(BF16)
    return high, middle, (rest - middle.astype(F32)).astype(BF16)


def times(a, b):
    return a[0] * b[0] - a[1] * b[1], a[0] * b[1] + a[1] * b[0]


def later(x, k, fill):
    return jnp.where(iota(TILE, 0) < CHUNKS - k, pltpu.roll(x, CHUNKS - k, 0), fill)


def earlier(x, k, fill):
    return jnp.where(iota(TILE, 0) >= k, pltpu.roll(x, k, 0), fill)


def power(tab_ref, g, n):
    return tuple(jnp.broadcast_to(tab_ref[g, c, n : n + 1], TILE) for c in range(2))


def entries(tab_ref, ktab_ref, g, head, entry):
    last = iota(TILE, 0) == CHUNKS - 1
    moved = times(power(tab_ref, g, 1), entry)
    scan = tuple(jnp.where(last, ktab_ref[0] * m, 0.0) for m in moved)
    if head is not None:
        scan = tuple(h + s for h, s in zip(head, scan))
    for n in range(3):
        near = tuple(later(x, 1 << n, 0.0) for x in scan)
        moved = times(power(tab_ref, g, 1 << n), near)
        scan = tuple(s + ktab_ref[n] * m for s, m in zip(scan, moved))
    return tuple(jnp.where(last, e, pltpu.roll(s, CHUNKS - 1, 0)) for e, s in zip(entry, scan))


def fold(x):
    block = (iota((SIZE, GROUP), 1) % LANES) // 32
    out = x[:SIZE]
    for j in range(1, 4):
        out = jnp.where(block == j, x[j * SIZE : (j + 1) * SIZE], out)
    return out


def walk(length, groups, units, states, keep_ref, load, store):
    for i in range(length - 1, -1, -1):
        at = pl.ds(i, CHUNKS, stride=length)
        keep = keep_ref[at, :]
        for n in range(groups):
            re, im = states[n]
            step_re, step_im = keep * units[n][0], keep * units[n][1]
            if load is None:
                states[n] = (step_re * re - step_im * im, step_re * im + step_im * re)
            else:
                a, b = load(n, at)
                states[n] = ((a + step_re * re) - step_im * im, (b + step_re * im) + step_im * re)
            if store is not None:
                store(n, at, states[n])
    return states


def basis_kernel(length, code_ref, reflect_ref, high_ref, low_ref, tab_ref, far_ref, u_ref, wide_ref):
    rows = reflect_ref.shape[0]
    blocks = rows // 4
    groups = blocks // 4

    wide_ref[...] = jnp.concatenate([code_ref[...]] * 4, axis=1)
    codes = wide_ref[pl.ds(0, groups, stride=4), :]
    block = iota(codes.shape, 1) // 32
    for j in range(1, 4):
        codes = jnp.where(block == j, wide_ref[pl.ds(j, groups, stride=4), :], codes)

    rates = jnp.exp(-math.log(2.0) * (4.0 + (codes & 1023).astype(F32) * (10.0 / 1024.0)))
    series = jnp.full_like(rates, 1.0 / 8.0)
    for k in range(7, 0, -1):
        series = series * rates + 1.0 / k
    logs = -rates * series
    angles = codes >> 10
    row = iota(TILE, 0)
    n = jnp.where(row == 0, 1, row * length)
    for g in range(groups):
        turn = ((n * angles[g : g + 1, :]) & 8191).astype(F32) * (math.pi / 4096.0)
        size = jnp.exp(n.astype(F32) * logs[g : g + 1, :])
        re, im = size * jnp.cos(turn), -size * jnp.sin(turn)
        tab_ref[g, 0] = re
        tab_ref[g, 1] = im
        half = (re[4:5], im[4:5])
        whole = times(half, half)
        far_ref[0, g : g + 1, :] = whole[0]
        far_ref[1, g : g + 1, :] = whole[1]

    v = [reflect_ref[pl.ds(k, blocks, stride=4), :] for k in range(4)]
    u = []
    for k in range(4):
        now = v[k]
        for l in range(k):
            now = now - u[l] * jnp.sum(v[l] * v[k], axis=1, keepdims=True)
        u.append(now * (2.0 / jnp.sum(v[k] * v[k], axis=1, keepdims=True)))
        u_ref[pl.ds(k, blocks, stride=4), :] = u[k]
    to = iota((SIZE, SIZE), 1)
    sort = jnp.where(iota((SIZE, SIZE), 0) == (to % 32) * 2 + to // 32, 1.0, 0.0).astype(F32)
    sorted_v = matmul(reflect_ref[...], sort, NN, lax.Precision.HIGHEST)
    wide = (rows, GROUP)
    block = (iota(wide, 0) // 4) % 4
    wide_v = jnp.concatenate([sorted_v[:, :32]] * 4 + [sorted_v[:, 32:]] * 4, axis=1)
    wide_v = split3(jnp.where(block == (iota(wide, 1) % LANES) // 32, wide_v, 0.0))
    wide_u = split3(jnp.where(block == iota(wide, 1) // SIZE, jnp.concatenate([u_ref[...]] * 4, axis=1), 0.0))
    to = iota((GROUP, GROUP), 1)
    order = jnp.where(iota((GROUP, GROUP), 0) == ((to % LANES) // 32) * SIZE + (to % 32) * 2 + to // LANES, 1.0, 0.0).astype(F32)
    for g in range(groups):
        at = slice(g * 16, (g + 1) * 16)
        left = jnp.concatenate([wide_u[n][at] for n in (0, 0, 1, 0, 1, 2)], axis=0)
        right = jnp.concatenate([wide_v[n][at] for n in (0, 1, 0, 2, 1, 0)], axis=0)
        high, low = split(order - matmul(left, right, TN))
        high_ref[g] = high
        low_ref[g] = low


def weight_kernel(length, boundary_ref, tab_ref, prev_ref, keep_ref, ktab_ref, turned_ref, decay_ref, weight_ref):
    groups = tab_ref.shape[0]
    keep = jnp.where(boundary_ref[...] == 1, 0.6, 1.0).astype(F32)
    keep_ref[...] = jnp.broadcast_to(keep, (LANES, keep.shape[1])).T

    chunk = keep_ref[pl.ds(0, CHUNKS, stride=length), :]
    for i in range(1, length):
        chunk = chunk * keep_ref[pl.ds(i, CHUNKS, stride=length), :]
    two = chunk * later(chunk, 1, 1.0)
    four = two * later(two, 2, 1.0)
    before = earlier(chunk, 1, 1.0)
    before = before * earlier(before, 1, 1.0)
    before = before * earlier(before, 2, 1.0)
    before = before * earlier(before, 4, 1.0)
    eight = four * later(four, 4, 1.0)
    ktab_ref[0] = chunk
    ktab_ref[1] = two
    ktab_ref[2] = four
    ktab_ref[3] = before
    ktab_ref[4] = jnp.broadcast_to(eight[0:1], TILE)

    one, zero = jnp.ones(TILE, F32), jnp.zeros(TILE, F32)
    for first in range(0, groups, 4):
        some = range(first, min(first + 4, groups))
        states = [entries(tab_ref, ktab_ref, g, None, (one, zero)) for g in some]
        units = [power(tab_ref, g, 0) for g in some]

        def store(k, at, state):
            decay_ref[first + k, 0, at, :] = state[0]
            decay_ref[first + k, 1, at, :] = state[1]

        walk(length, len(some), units, states, keep_ref, None, store)
    for g in range(groups):
        columns = slice(g * GROUP, (g + 1) * GROUP)
        turned = prev_ref[:, columns].T
        turned_ref[columns, :] = turned
        high, low = split(jnp.concatenate([decay_ref[g, 0], decay_ref[g, 1]], axis=1))
        weight_ref[g] = fold(matmul(turned, high) + matmul(turned, low))


VMEM = pl.BlockSpec(memory_space=pltpu.VMEM)
SMEM = pl.BlockSpec(memory_space=pltpu.SMEM)
HBM = pl.BlockSpec(memory_space=pltpu.HBM)


def call(kernel, out_shape, args, specs, scratch=(), flops=0):
    shapes = [jax.ShapeDtypeStruct(s, t) for s, t in out_shape]
    moved = sum(a.size * a.dtype.itemsize for a in args) + sum(s.size * s.dtype.itemsize for s in shapes)
    return pl.pallas_call(
        kernel,
        out_shape=shapes,
        in_specs=specs,
        out_specs=[VMEM] * len(shapes),
        scratch_shapes=list(scratch),
        compiler_params=pltpu.CompilerParams(vmem_limit_bytes=LIMIT),
        cost_estimate=pl.CostEstimate(flops=int(flops), bytes_accessed=int(moved), transcendentals=0),
    )(*args)


def basis(code, reflect, length):
    blocks = reflect.shape[0]
    groups = blocks // 4
    out = [
        ((groups, GROUP, GROUP), BF16),
        ((groups, GROUP, GROUP), BF16),
        ((groups, 2) + TILE, F32),
        ((2, groups, LANES), F32),
    ]
    args = (code, reflect.reshape(blocks * 4, SIZE))
    scratch = [pltpu.VMEM((blocks * 4, SIZE), F32), pltpu.VMEM((blocks, LANES), jnp.int32)]
    return call(functools.partial(basis_kernel, length), out, args, [VMEM] * 2, scratch, groups * 2 * 2 * 256**3)


def weights(boundary, tab, prev):
    groups = tab.shape[0]
    tokens, channels = prev.shape
    out = [
        ((tokens, LANES), F32),
        ((5,) + TILE, F32),
        ((channels, tokens), BF16),
        ((groups, 2, tokens, LANES), F32),
        ((groups, SIZE, GROUP), F32),
    ]
    return call(functools.partial(weight_kernel, tokens // CHUNKS), out, (boundary, tab, prev), [VMEM] * 3, (), groups * 2 * 2 * 256**3)


def scan_kernel(length, base, count, peers, begin, finish, aheads, *refs):
    refs = list(refs)
    take = lambda n: [refs.pop(0) for _ in range(n)]
    tab_ref, ktab_ref, keep_ref = take(3)
    if begin:
        place_ref, own_ref, high_ref, low_ref = take(4)
        others = take(peers - 1)
    if begin and not finish:
        ahead = take(aheads)
    if finish:
        (turned_ref,) = take(1)
    if begin:
        out_ref, head_ref, first_ref = take(3) if not finish else take(1) + [None] + take(1)
    else:
        in_ref, head_ref, out_ref = take(3)
    if finish:
        (grad_ref,) = take(1)
    heads = []
    if begin:
        place = place_ref[0]
        if finish:
            rows_ref, spaced_ref = take(2)
            size = own_ref.shape[0]
            width = count * GROUP
            channels = high_ref.shape[0] * GROUP
            at = [pl.ds(pl.multiple_of((place ^ k) * size, size), size) for k in range(peers)]
            rows_ref[at[0], :] = own_ref[:, pl.ds(pl.multiple_of(place * channels + base * GROUP, GROUP), width)]
            for k in range(1, peers):
                rows_ref[at[k], :] = others[k - 1][...]
            for n in range(count):
                rows = rows_ref[:, n * GROUP : (n + 1) * GROUP]
                out = matmul(rows, high_ref[base + n]) + matmul(rows, low_ref[base + n])
                spaced_ref[n, 0] = out[:, :LANES]
                spaced_ref[n, 1] = out[:, LANES:]
        else:
            spaced_ref = out_ref
            size = own_ref.shape[2]
            at = [pl.ds(pl.multiple_of((place ^ k) * size, size), size) for k in range(peers)]
            for n in range(count):
                for c in range(2):
                    spaced_ref[n, c, at[0], :] = own_ref[n, c]
                for k in range(1, peers):
                    rows = others[k - 1][:, n * GROUP : (n + 1) * GROUP]
                    out = matmul(rows, high_ref[base + n]) + matmul(rows, low_ref[base + n])
                    spaced_ref[n, 0, at[k], :] = out[:, :LANES]
                    spaced_ref[n, 1, at[k], :] = out[:, LANES:]
    else:
        spaced_ref = in_ref
    load = lambda n, at: (spaced_ref[n, 0, at, :], spaced_ref[n, 1, at, :])
    units = [power(tab_ref, base + n, 0) for n in range(count)]
    zero = jnp.zeros(TILE, F32)
    if begin and not finish:
        groups = base + count
        at = 0
        for ref in ahead:
            size = ref.shape[1]
            for c in range(2):
                first_ref[c * groups + at : c * groups + at + size, :] = ref[c]
            at += size
        first_ref[2 * groups :, :] = ktab_ref[4]
    if begin:
        heads = walk(length, count, units, [(zero, zero)] * count, keep_ref, load, None)
        before = ktab_ref[3]
        for n in range(count):
            if head_ref is not None:
                head_ref[n, 0] = heads[n][0]
                head_ref[n, 1] = heads[n][1]
            hop = tuple(jnp.where(iota(TILE, 0) == 0, one, tab_ref[base + n, c]) for c, one in ((0, 1.0), (1, 0.0)))
            moved = times(hop, heads[n])
            for c in range(2):
                value = jnp.sum(moved[c] * before, axis=0, keepdims=True)
                if finish:
                    first_ref[c, n : n + 1, :] = value
                else:
                    first_ref[c * groups + base + n : c * groups + base + n + 1, :] = value
    else:
        heads = [(head_ref[n, 0], head_ref[n, 1]) for n in range(count)]
    if finish:
        states = [entries(tab_ref, ktab_ref, base + n, heads[n], (zero, zero)) for n in range(count)]

        def store(n, at, state):
            out_ref[n, 0, at, :] = state[0]
            out_ref[n, 1, at, :] = state[1]

        walk(length, count, units, states, keep_ref, load, store)
        for n in range(count):
            high, low = split(jnp.concatenate([out_ref[n, 0], out_ref[n, 1]], axis=1))
            turned = turned_ref[(base + n) * GROUP : (base + n + 1) * GROUP, :]
            grad_ref[n] = fold(matmul(turned, high) + matmul(turned, low))


def ahead_kernel(base, place_ref, own_ref, high_ref, low_ref, out_ref):
    start = place_ref[0] * (high_ref.shape[0] * GROUP) + base * GROUP
    for n in range(out_ref.shape[0]):
        rows = own_ref[:, pl.ds(pl.multiple_of(start + n * GROUP, GROUP), GROUP)]
        out = matmul(rows, high_ref[base + n]) + matmul(rows, low_ref[base + n])
        out_ref[n, 0] = out[:, :LANES]
        out_ref[n, 1] = out[:, LANES:]


def ahead_rows(base, count, place, rows, high, low):
    return call(functools.partial(ahead_kernel, base), [((count, 2, rows.shape[0], LANES), F32)], (place, rows, high, low),
                [SMEM] + [VMEM] * 3, (), count * 2 * 256**3)[0]


def scan_both(base, count, place, rows, parts, high, low, tab, ktab, keep, turned):
    tokens = keep.shape[0]
    peers = len(parts) + 1
    out = [((count, 2, tokens, LANES), F32), ((2, count, LANES), F32), ((count, SIZE, GROUP), F32)]
    return call(functools.partial(scan_kernel, tokens // CHUNKS, base, count, peers, True, True, 0), out,
                (tab, ktab, keep, place, rows, high, low, *parts, turned), [VMEM] * 3 + [SMEM] + [VMEM] * (peers + 3),
                [pltpu.VMEM((tokens, count * GROUP), BF16), pltpu.VMEM((count, 2, tokens, LANES), F32)], count * 4 * 2 * 256**3)


def scan_first(base, count, place, rows, parts, high, low, tab, ktab, keep, ahead):
    tokens = keep.shape[0]
    peers = len(parts) + 1
    out = [((count, 2, tokens, LANES), F32), ((count, 2) + TILE, F32), ((2 * (base + count) + CHUNKS, LANES), F32)]
    return call(functools.partial(scan_kernel, tokens // CHUNKS, base, count, peers, True, False, len(ahead)), out,
                (tab, ktab, keep, place, rows, high, low, *parts, *ahead), [VMEM] * 3 + [SMEM] + [VMEM] * (peers + 2 + len(ahead)),
                (), count * 2 * 2 * 256**3)


def scan_second(base, count, spaced, head, tab, ktab, keep, turned):
    tokens = keep.shape[0]
    out = [((count, 2, tokens, LANES), F32), ((count, SIZE, GROUP), F32)]
    return call(functools.partial(scan_kernel, tokens // CHUNKS, base, count, 0, False, True, 0), out,
                (tab, ktab, keep, turned, spaced, head), [VMEM] * 6, (), count * 2 * 2 * 256**3)


def state_kernel(base, sizes, entry_ref, decay_ref, high_ref, low_ref, *refs):
    parts, out_ref = refs[: len(sizes)], refs[-1]
    g = pl.program_id(0) + base
    re, im = entry_ref[0, pl.ds(g, 1), :], entry_ref[1, pl.ds(g, 1), :]
    d_re, d_im = decay_ref[0, 0], decay_ref[0, 1]
    z_re, z_im = parts[0][0, 0], parts[0][0, 1]
    start = 0
    for size, part in zip(sizes[:-1], parts[1:]):
        start += size
        z_re, z_im = jnp.where(g < start, z_re, part[0, 0]), jnp.where(g < start, z_im, part[0, 1])
    z_re = z_re + (re * d_re - im * d_im)
    z_im = z_im + (re * d_im + im * d_re)
    z_high, z_low = split(jnp.concatenate([z_re, z_im], axis=1))
    out = matmul(z_high, high_ref[0], NT) + matmul(z_high, low_ref[0], NT) + matmul(z_low, high_ref[0], NT)
    out_ref[...] = out.astype(BF16)


def states(base, count, parts, decay, entry, high, low, filled=None):
    groups = high.shape[0]
    tokens = parts[0].shape[2]
    sizes = [part.shape[0] for part in parts]
    each = lambda shape: pl.BlockSpec((1,) + shape, lambda g: (g + base, 0, 0, 0)[: len(shape) + 1])

    def pick(start, size):
        return pl.BlockSpec((1, 2, tokens, LANES), lambda g: (jnp.minimum(jnp.maximum(g + base - start, 0), size - 1), 0, 0, 0))

    args = [entry, decay, high, low, *parts]
    specs = [pl.BlockSpec(entry.shape, lambda g: (0, 0, 0)), each((2, tokens, LANES)), each((GROUP, GROUP)), each((GROUP, GROUP))]
    specs += [pick(sum(sizes[:n]), size) for n, size in enumerate(sizes)]
    alias = {}
    if filled is not None:
        alias = {len(args): 0}
        args.append(filled)
        specs.append(pl.BlockSpec(memory_space=pl.ANY))
    return pl.pallas_call(
        functools.partial(state_kernel, base, sizes),
        grid=(count,),
        in_specs=specs,
        out_specs=pl.BlockSpec((tokens, GROUP), lambda g: (0, g + base)),
        out_shape=jax.ShapeDtypeStruct((tokens, groups * GROUP), BF16),
        input_output_aliases=alias,
        name="states",
        compiler_params=pltpu.CompilerParams(vmem_limit_bytes=LIMIT),
        cost_estimate=pl.CostEstimate(flops=count * 3 * 2 * 256**3, bytes_accessed=count * 900_000, transcendentals=0),
    )(*args)


STEPS = 32000.0
LEAST = -100


def encode(x, code_ref):
    most = jnp.max(jnp.abs(x), axis=0, keepdims=True)
    power = jnp.ceil(jnp.log2(jnp.maximum(most, 2.0**LEAST)))
    code = jnp.floor(x * (jnp.exp2(-power) * STEPS) + 0.5).astype(jnp.int32)
    row = iota((16, x.shape[1]), 0)
    bit = ((power - LEAST).astype(jnp.int32) >> row) & 1
    first = jnp.where(row < 8, (code[:16] & -2) | bit, code[:16])
    code_ref[:16, :] = first.astype(jnp.int16)
    code_ref[16:, :] = code[16:].astype(jnp.int16)


def decode(code_ref, start=0, rows=None):
    rows = code_ref.shape[0] if rows is None else rows
    first = code_ref[start : start + 16, :].astype(jnp.int32)
    row = iota(first.shape, 0)
    bits = jnp.where(row < 8, (first & 1) << row, 0).astype(F32)
    power = jnp.sum(bits, axis=0, keepdims=True) + float(LEAST)
    return code_ref[start : start + rows, :].astype(jnp.int32).astype(F32) * (jnp.exp2(power) * (1.0 / STEPS))


def merge_kernel(half, side_ref, bit_ref, entry_ref, weight_ref, *refs):
    parts, outs, (own_ref, away_ref) = refs[:-6], refs[-6:-2], refs[-2:]
    blocks = [part.at[n] for part in parts for n in range(part.shape[0])]
    side, bit = side_ref[0], bit_ref[0]
    for n in range(half):
        for out_ref, which in ((own_ref, side), (away_ref, 1 - side)):
            here = jnp.where(which == 0, blocks[n][...], blocks[half + n][...])
            at = which * half + n
            re, im = entry_ref[0, pl.ds(at, 1), :], entry_ref[1, pl.ds(at, 1), :]
            weight = weight_ref[at]
            w_re, w_im = weight[:, :LANES], weight[:, LANES:]
            out_ref[n * SIZE : (n + 1) * SIZE, :LANES] = here[:, :LANES] + (re * w_re - im * w_im)
            out_ref[n * SIZE : (n + 1) * SIZE, LANES:] = here[:, LANES:] + (re * w_im + im * w_re)
    rows = half * SIZE // 2
    here, there = (pl.ds(pl.multiple_of(n * rows, rows), rows) for n in (bit, 1 - bit))
    outs[0][...] = own_ref[here, :]
    outs[1][...] = own_ref[there, :]
    encode(away_ref[here, :], outs[2])
    encode(away_ref[there, :], outs[3])


def merge(half, side, bit, entry, weight, parts):
    rows = half * SIZE // 2
    out = [((rows, GROUP), F32)] * 2 + [((rows, GROUP), jnp.dtype(jnp.int16))] * 2
    return call(functools.partial(merge_kernel, half), out, (side, bit, entry, weight, *parts),
                [SMEM] * 2 + [VMEM] * (2 + len(parts)), [pltpu.VMEM((half * SIZE, GROUP), F32)] * 2)


def add_kernel(*refs):
    total = None
    for ref in refs[:-1]:
        term = ref[...] if ref.dtype == F32 else decode(ref)
        total = term if total is None else total + term
    encode(total, refs[-1])


def add(*terms):
    return call(add_kernel, [(terms[-1].shape, terms[-1].dtype)], terms, [VMEM] * len(terms))[0]


def final_kernel(flips, quarters, side_ref, bit_ref, x_ref, high_ref, low_ref, *refs):
    out_hbm, out_ref, sems = refs[-3:]
    half = high_ref.shape[0] // 2
    count = half * quarters // 2
    side, bit = (1 - ref[0] if flip else ref[0] for ref, flip in zip((side_ref, bit_ref), flips))
    start = side * half + bit * count if quarters == 1 else side * half
    rows = x_ref.shape[0] // quarters
    x = jnp.concatenate([decode(x_ref, n * rows, rows) for n in range(quarters)], axis=0)
    copies = []
    for n in range(count):
        at = start + n
        x_high, x_low = split(x[n * SIZE : (n + 1) * SIZE, :])
        out = matmul(high_ref[at], x_high, NT) + matmul(low_ref[at], x_high, NT) + matmul(high_ref[at], x_low, NT)
        for j in range(4):
            out_ref[4 * n + j] = out[j * SIZE : (j + 1) * SIZE]
        copies.append(pltpu.make_async_copy(out_ref.at[pl.ds(4 * n, 4)], out_hbm.at[pl.ds(at * 4, 4)], sems.at[n]))
        copies[-1].start()
    for copy in copies:
        copy.wait()


def final(flips, quarters, side, bit, x, high, low, filled=None):
    count = high.shape[0] // 2 * quarters // 2
    blocks = high.shape[0] * 4
    args = [side, bit, x, high, low]
    specs = [SMEM] * 2 + [VMEM] * 3
    alias = {}
    if filled is not None:
        alias = {len(args): 0}
        args.append(filled)
        specs.append(HBM)
    return pl.pallas_call(
        functools.partial(final_kernel, flips, quarters),
        out_shape=jax.ShapeDtypeStruct((blocks, SIZE, SIZE), F32),
        in_specs=specs,
        out_specs=HBM,
        scratch_shapes=[pltpu.VMEM((4 * count, SIZE, SIZE), F32), pltpu.SemaphoreType.DMA((count,))],
        input_output_aliases=alias,
        name="final",
        compiler_params=pltpu.CompilerParams(vmem_limit_bytes=LIMIT),
        cost_estimate=pl.CostEstimate(flops=count * 3 * 2 * 256 * 256 * 64, bytes_accessed=count * 400_000, transcendentals=0),
    )(*args)


def swap(x, axis, k):
    n = lax.axis_size(axis)
    return lax.ppermute(x, axis, [(i, i ^ k) for i in range(n)])


def entering(sent, far, axis, early_bits):
    peers = lax.axis_size(axis)
    rows = far[0].shape[0]
    first, total = (sent[:rows], sent[rows : 2 * rows]), sent[2 * rows : 2 * rows + 1]
    entry = (jnp.zeros_like(first[0]), jnp.zeros_like(first[1]))
    gap = (jnp.ones_like(first[0]), jnp.zeros_like(first[0]))
    k = 1
    for early in early_bits:
        if k > 1:
            sent = jnp.concatenate([first[0], first[1], jnp.broadcast_to(total, (8, LANES))])
        got = swap(sent, axis, k)
        other = (got[:rows], got[rows : 2 * rows])
        other_total = got[2 * rows : 2 * rows + 1]
        reach = times(gap, other)
        entry = tuple(jnp.where(early, e + r, e) for e, r in zip(entry, reach))
        if 2 * k < peers:
            step = times(gap, far)
            gap = tuple(jnp.where(early, other_total * s, g) for s, g in zip(step, gap))
            near = tuple(jnp.where(early, a, b) for a, b in zip(first, other))
            late = tuple(jnp.where(early, b, a) for a, b in zip(first, other))
            moved = times(far, late)
            first = tuple(a + jnp.where(early, total, other_total) * b for a, b in zip(near, moved))
            total = total * other_total
            far = times(far, far)
        k *= 2
    return jnp.stack(entry)


def exchanges(axes):
    steps = []
    for axis in axes:
        k = 1
        while k < lax.axis_size(axis):
            steps.append((axis, k))
            k *= 2
    return steps


def bits(steps):
    return [(lax.axis_index(axis).astype(jnp.uint32) // jnp.uint32(k)) & jnp.uint32(1) for axis, k in steps]


def total_sum(quarters, steps):
    own_here, own_there, away_here, away_there = quarters
    got = swap(away_there, *steps[0])
    code = add(own_there, got)
    near = swap(away_here, *steps[0])
    got = swap(code, *steps[1])
    code = add(own_here, near, got)
    for step in steps[2:]:
        got = swap(code, *step)
        code = add(code, got)
    return code


def spread(code, steps, side, bit, lower, high, low):
    other = swap(code, *steps[1])
    if high.shape[0] % 4:
        both = jnp.where(lower, jnp.concatenate([code, other]), jnp.concatenate([other, code]))
        away = swap(both, *steps[0])
        out = final((False, False), 2, side, bit, both, high, low)
        return final((True, False), 2, side, bit, away, high, low, out)
    near = swap(code, *steps[0])
    out = final((False, False), 1, side, bit, code, high, low)
    out = final((True, False), 1, side, bit, near, high, low, out)
    far = swap(other, *steps[0])
    out = final((False, True), 1, side, bit, other, high, low, out)
    return final((True, True), 1, side, bit, far, high, low, out)


def inner(out_grad, prev_state, boundary, angle_code, radius_code, reflect):
    peers, place = lax.axis_size("tensor"), lax.axis_index("tensor")
    rows = out_grad[0]
    channels = prev_state.shape[2]
    tokens = prev_state.shape[1]
    groups = channels // GROUP
    half = groups // 2
    counts = [max(1, groups * 5 // 8)]
    counts.append(groups - counts[0])
    bases = [sum(counts[:n]) for n in range(len(counts))]
    place = place.astype(jnp.uint32)

    def away(k, base, count):
        start = (place ^ jnp.uint32(k)) * jnp.uint32(channels) + jnp.uint32(base * GROUP)
        return lax.dynamic_slice(rows, (jnp.uint32(0), start), (rows.shape[0], count * GROUP))

    parts = []
    for at in zip(bases, counts):
        parts.append([swap(away(k, *at), "tensor", k) for k in range(1, peers)])
    steps = exchanges(("dp", "ctx"))
    bit = bits(steps)[1]
    lower = bit == 0
    bit = jnp.reshape(bit.astype(jnp.int32), (1,))
    side = jnp.reshape(lax.axis_index("dp") & 1, (1,))
    place = jnp.reshape(place.astype(jnp.int32), (1,))
    early = [bit == 0 for bit in bits(exchanges(("ctx",)))]
    code = angle_code * 1024 + radius_code
    code, side, place, bit, lower, early = lax.optimization_barrier((code, side, place, bit, lower, early))
    high, low, tab, far = basis(code, reflect, tokens // CHUNKS)
    keep, ktab, turned, decay, weight = weights(boundary, tab, prev_state[0])
    ahead = ahead_rows(bases[-1], counts[-1], place, rows, high, low)
    done = []
    for base, count, part in zip(bases[:-1], counts[:-1], parts[:-1]):
        done.append(scan_both(base, count, place, rows, part, high, low, tab, ktab, keep, turned))
    base, count = bases[-1], counts[-1]
    spaced, head, sent = scan_first(base, count, place, ahead, parts[-1], high, low, tab, ktab, keep, [d[1] for d in done])
    entry = entering(sent, (far[0], far[1]), "ctx", early)
    z_last, grad_last = scan_second(base, count, spaced, head, tab, ktab, keep, turned)
    quarters = merge(half, side, bit, entry, weight, [d[2] for d in done] + [grad_last])
    z = [d[0] for d in done] + [z_last]
    grad_input = None
    for base, count in shares(groups):
        if count:
            grad_input = states(base, count, z, decay, entry, high, low, grad_input)
    grad_transition = spread(total_sum(quarters, steps), steps, side, bit, lower, high, low)
    return grad_input[None], grad_transition


def shares(groups):
    counts = [groups // 4]
    counts.append((groups - counts[0] + 1) // 2)
    counts.append(groups - sum(counts))
    return [(sum(counts[:n]), count) for n, count in enumerate(counts)]


def solution(mesh):
    in_specs = (
        P("dp", ("ctx", "tensor"), None),
        P("dp", "ctx", "tensor"),
        P("dp", "ctx"),
        P("tensor", None),
        P("tensor", None),
        P("tensor", None, None),
    )
    out_specs = (P("dp", "ctx", "tensor"), P("tensor", None, None))
    return jax.shard_map(inner, mesh=mesh, in_specs=in_specs, out_specs=out_specs, check_vma=False)
```
